128 devices in a mesh: gx: 16 (over z, y), gy: 8 (over x, core).
Axes of the slice: x: 4, y: 4, z: 4, core: 2. Of those that a mesh axis runs over, the one named last changes fastest.
Arguments:
- jacobian: bfloat16 [16384, 192, 384], P(('gx', 'gy')), may hold values from -0.3125 to 0.3125
- grain_slots: int32 [16384, 64], P(('gx', 'gy')), may hold values from 0 to 18431, as said below
- block_count: int32 [128], P(('gx', 'gy')), may hold values from 1 to 128, as said below
- impulse_start: float32 [16384, 192], P(('gx', 'gy')), may hold values from -3 to 3
- velocity_bias: float32 [16384, 192], P(('gx', 'gy')), may hold values from -6 to 6
- friction: float32 [16384, 64], P(('gx', 'gy')), may hold values from 0.2 to 0.8
- free_velocity: float32 [6, 262144], P(None, ('gx', 'gy')), may hold values from -6 to 6
- inverse_mass: float32 [6, 262144], P(None, ('gx', 'gy')), may hold values from 0.5 to 4
Outputs:
- impulses: float32 [16384, 192], P(('gx', 'gy'))
- velocities: float32 [6, 262144], P(None, ('gx', 'gy'))
The draws below stay inside these ranges and needn't reach their ends.
Inputs may be any that keep to these rules, and one draw needn't show every extreme that they name: `grain_slots`: A slot value s * 2048 + l names grain l of the device at offset (s // 3 - 1, s % 3 - 1) along (gx, gy) from the block's device (the device holding the block's row); that device always exists. A device's first block_count block slots are live, the rest are not; some device has all 128 live.
All inputs are finite; a program needn't handle non-finite values.
Results may differ from the reference program's by a relative error of at most 0.014.
Values may be sent and summed in bfloat16 or wider, within the bound.
A program may use at most 128 MiB of HBM per device.

```python
import math
import jax
import jax.numpy as jnp
from jax import lax

CB = 64
GB = 64
BLK_DEV = 128
GRAIN_DEV = 2048
ITERS = 3
NBLK = 16384
NGRAIN = 262144
N_GX = 16
N_GY = 8


def draw_grain_slots(key, part):
    key = jax.random.fold_in(key, 11)
    key_one, key_two, key_three = jax.random.split(key, 3)
    blocks = BLK_DEV * N_GX * N_GY
    device = jnp.arange(blocks, dtype=jnp.int32) // BLK_DEV
    row_x = (device // N_GY)[:, None]
    row_y = (device % N_GY)[:, None]
    step_x = jax.random.randint(key_one, (blocks, GB), -1, 2)
    step_y = jax.random.randint(key_two, (blocks, GB), -1, 2)
    step_x = jnp.where((row_x + step_x < 0) | (row_x + step_x >= N_GX), 0, step_x)
    step_y = jnp.where((row_y + step_y < 0) | (row_y + step_y >= N_GY), 0, step_y)
    local_grain = jax.random.randint(key_three, (blocks, GB), 0, GRAIN_DEV)
    slot_table = ((step_x + 1) * 3 + (step_y + 1)) * GRAIN_DEV + local_grain
    slot_table = slot_table.at[0, 0].set(9 * GRAIN_DEV - 1)
    slot_table = slot_table.at[blocks - 1, 0].set(0)
    return slot_table.astype(jnp.int32)


def draw_block_count(key, part):
    key = jax.random.fold_in(key, 23)
    key_one, key_two = jax.random.split(key)
    devices = N_GX * N_GY
    row_y = jnp.arange(devices, dtype=jnp.int32) % N_GY
    upper_bound = BLK_DEV // 4 + (BLK_DEV - BLK_DEV // 4) * row_y // (N_GY - 1)
    lower_bound = jnp.maximum(1, upper_bound // 2)
    counts = jax.random.randint(key_one, (devices,), lower_bound, upper_bound + 1)
    chosen = jax.random.randint(key_two, (), 0, N_GX)
    counts = counts.at[chosen * N_GY + N_GY - 1].set(BLK_DEV)
    return counts.astype(jnp.int32)


def shard_levels(stream_key, dims, shards, least, top_value):
    def one(position, parts):
        steps = jax.random.uniform(jax.random.fold_in(jax.random.fold_in(stream_key, 6), position), (parts,), jnp.float32, least / len(shards), top_value / len(shards))
        return jnp.repeat(jnp.exp(steps), dims[position] // parts).reshape((-1,) + (1,) * (len(dims) - position - 1))

    level = one(*shards[0])
    for cut in shards[1:]:
        level = level * one(*cut)
    return level


def normal_values(own_key, dims, scale, limit, pieces=(), kind=jnp.bfloat16):
    factor_of = shard_levels(own_key, dims, pieces, -0.22, 0.18) if pieces else 1.0
    result = jax.random.normal(own_key, dims, jnp.float32) * scale * factor_of
    return jnp.minimum(jnp.maximum(result, -limit), limit).astype(kind)


def setup_inputs(seed: int = 0) -> dict:
    seeds = jax.random.split(jax.random.key(seed), 9)
    jacobian = normal_values(seeds[0], (NBLK, 3 * CB, 6 * GB), (6 * GB) ** -0.5, 0.3125, ((0, 128),))
    grain_slots = draw_grain_slots(jax.random.fold_in(seeds[8], 71), 0)
    block_count = draw_block_count(jax.random.fold_in(seeds[8], 71), 0)
    impulse_start = normal_values(seeds[3], (NBLK, 3 * CB), 0.5, 3.0, ((0, 128),), jnp.float32)
    velocity_bias = normal_values(seeds[4], (NBLK, 3 * CB), 1.0, 6.0, ((0, 128),), jnp.float32)
    friction = jnp.clip(0.2 + 0.6 * jax.random.uniform(seeds[5], (NBLK, CB), jnp.float32) ** shard_levels(seeds[5], (NBLK, CB), ((0, 128),), -0.2, 0.2), 0.2, 0.8)
    free_velocity = normal_values(seeds[6], (6, NGRAIN), 1.0, 6.0, ((1, 128),), jnp.float32)
    inverse_mass = jnp.clip(jnp.exp(math.log(4.0) - 2.0794415 * jax.random.uniform(seeds[7], (6, NGRAIN), jnp.float32) ** shard_levels(seeds[7], (6, NGRAIN), ((1, 128),), -0.2, 0.2)), 0.5, 4.0)
    return dict(jacobian=jacobian, grain_slots=grain_slots, block_count=block_count, impulse_start=impulse_start, velocity_bias=velocity_bias, friction=friction, free_velocity=free_velocity, inverse_mass=inverse_mass)


epsilon = 1e-06

def momentum_weights(iterations):
    momentum = 1.0
    weights = []
    for iteration in range(iterations):
        upcoming = (-momentum * momentum + momentum * math.sqrt(momentum * momentum + 4.0)) / 2.0
        weights.append(momentum * (1.0 - momentum) / (momentum * momentum + upcoming))
        momentum = upcoming
    return weights

def project_cone(target, friction):
    normal = target[:, :CB]
    tangent_one = target[:, CB:2 * CB]
    tangent_two = target[:, 2 * CB:]
    tangent_norm = jnp.sqrt(tangent_one * tangent_one + tangent_two * tangent_two)
    inside = tangent_norm <= friction * normal
    opposite = friction * tangent_norm <= -normal
    cone_normal = (normal + friction * tangent_norm) / (1.0 + friction * friction)
    cone_ratio = friction * cone_normal / jnp.where(tangent_norm > 0, tangent_norm, 1.0)
    new_normal = jnp.where(inside, normal, jnp.where(opposite, 0.0, cone_normal))
    shrink = jnp.where(inside, 1.0, jnp.where(opposite, 0.0, cone_ratio))
    return jnp.concatenate([new_normal, tangent_one * shrink, tangent_two * shrink], axis=1)

def make_index(grain_slots):
    blocks = grain_slots.shape[0]
    device = jnp.arange(blocks, dtype=jnp.int32) // BLK_DEV
    row_x = (device // N_GY)[:, None]
    row_y = (device % N_GY)[:, None]
    section = grain_slots // GRAIN_DEV
    local_grain = grain_slots % GRAIN_DEV
    owner = (row_x + section // 3 - 1) * N_GY + row_y + section % 3 - 1
    return (owner * GRAIN_DEV + local_grain).astype(jnp.int32)

def forward(jacobian, grain_index, grain_field):
    blocks = jacobian.shape[0]
    devices = N_GX * N_GY
    picked = jnp.transpose(grain_field[:, grain_index], (1, 0, 2)).reshape(blocks, 6 * GB)
    jacobian_split = jacobian.reshape(devices, BLK_DEV, 3 * CB, 6 * GB)
    picked_split = picked.reshape(devices, BLK_DEV, 6 * GB)

    def per_device(operands):
        return jnp.einsum('bij,bj->bi', operands[0].astype(jnp.float32), operands[1].astype(jnp.float32))
    return lax.map(per_device, (jacobian_split, picked_split)).reshape(blocks, 3 * CB)

def backward(jacobian, grain_index, impulse_field, grains_total):
    blocks = jacobian.shape[0]
    devices = N_GX * N_GY
    jacobian_split = jacobian.reshape(devices, BLK_DEV, 3 * CB, 6 * GB)
    impulse_split = impulse_field.reshape(devices, BLK_DEV, 3 * CB)

    def per_device(operands):
        return jnp.einsum('bij,bi->bj', operands[0].astype(jnp.float32), operands[1].astype(jnp.float32))
    pushes = lax.map(per_device, (jacobian_split, impulse_split)).reshape(blocks, 6, GB)
    pushes = jnp.transpose(pushes, (1, 0, 2))
    return jnp.zeros((6, grains_total), jnp.float32).at[:, grain_index].add(pushes)

def reference(jacobian, grain_slots, block_count, impulse_start, velocity_bias, friction, free_velocity, inverse_mass):
    blocks = jacobian.shape[0]
    grains_total = free_velocity.shape[1]
    grain_index = make_index(grain_slots)
    block_ids = jnp.arange(blocks, dtype=jnp.int32)
    live_mask = (block_ids % BLK_DEV < block_count[block_ids // BLK_DEV]).astype(jnp.float32)[:, None]
    constraint_bias = velocity_bias + forward(jacobian, grain_index, free_velocity.astype(jnp.bfloat16))
    extrapolated = impulse_start * live_mask
    previous = extrapolated
    current = extrapolated
    weights = momentum_weights(ITERS)
    for iteration in range(ITERS):
        pushed = backward(jacobian, grain_index, extrapolated.astype(jnp.bfloat16), grains_total)
        moved = inverse_mass * pushed
        size_total = jnp.sum(extrapolated * extrapolated)
        energy_total = jnp.sum(pushed * moved)
        gradient = (forward(jacobian, grain_index, moved.astype(jnp.bfloat16)) + constraint_bias) * live_mask
        step_size = size_total / (energy_total + epsilon)
        current = project_cone(extrapolated - step_size * gradient, friction) * live_mask
        extrapolated = current + weights[iteration] * (current - previous)
        previous = current
    final_push = backward(jacobian, grain_index, current.astype(jnp.bfloat16), grains_total)
    return (current, free_velocity + inverse_mass * final_push)
```

```python
import math

import jax
import jax.numpy as jnp
from jax import lax
from jax.sharding import Mesh
from jax.sharding import PartitionSpec as P

CB = 64
GB = 64
ITERS = 3
GX_GY = ("gx_0", "gx_1", "gy_0", "gy_1")
GX = ("gx_0", "gx_1")
GY = ("gy_0", "gy_1")


epsilon = 1e-06


def with_halo(array, sides, width):
    for axis, dim in sides:
        size, length = (lax.axis_size(axis), array.shape[dim])
        up = [(i, (i + 1) % size) for i in range(size - 1)]
        down = [(j, i) for i, j in up]
        last = lax.slice_in_dim(array, length - width, length, axis=dim)
        leading = lax.slice_in_dim(array, 0, width, axis=dim)
        before = lax.ppermute(last, axis, up)
        after = lax.ppermute(leading, axis, down)
        array = jnp.concatenate([before, array, after], axis=dim)
    return array


def from_behind(block, axis, distance):
    devices = range(lax.axis_size(axis))
    route = [(i - distance, i) for i in devices if i - distance in devices]
    return lax.ppermute(block, axis, route)


def one_axis_at_a_time(array, axes):
    for axis in axes:
        array = lax.psum(array, axis)
    return array


def momentum_weights(iterations):
    momentum = 1.0
    weights = []
    for iteration in range(iterations):
        upcoming = (-momentum * momentum + momentum * math.sqrt(momentum * momentum + 4.0)) / 2.0
        weights.append(momentum * (1.0 - momentum) / (momentum * momentum + upcoming))
        momentum = upcoming
    return weights


def project_cone(target, friction):
    normal = target[:, :CB]
    tangent_one = target[:, CB : 2 * CB]
    tangent_two = target[:, 2 * CB :]
    tangent_norm = jnp.sqrt(tangent_one * tangent_one + tangent_two * tangent_two)
    inside = tangent_norm <= friction * normal
    opposite = friction * tangent_norm <= -normal
    cone_normal = (normal + friction * tangent_norm) / (1.0 + friction * friction)
    cone_ratio = friction * cone_normal / jnp.where(tangent_norm > 0, tangent_norm, 1.0)
    new_normal = jnp.where(inside, normal, jnp.where(opposite, 0.0, cone_normal))
    shrink = jnp.where(inside, 1.0, jnp.where(opposite, 0.0, cone_ratio))
    return jnp.concatenate([new_normal, tangent_one * shrink, tangent_two * shrink], axis=1)


def shards(
    jacobian,
    grain_slots,
    block_count,
    impulse_start,
    velocity_bias,
    friction,
    free_velocity,
    inverse_mass,
):
    blocks = jacobian.shape[0]
    grains = free_velocity.shape[1]
    live_mask = (jnp.arange(blocks, dtype=jnp.int32) < block_count[0]).astype(jnp.float32)[:, None]

    def forward(grain_field):
        nearby = with_halo(grain_field.reshape(6, 1, 1, grains), ((GX, 1), (GY, 2)), 1)
        nearby = nearby.reshape(6, 9 * grains)
        picked = jnp.take(nearby, grain_slots, axis=1)
        picked = jnp.transpose(picked, (1, 0, 2)).reshape(blocks, 6 * GB)
        return jnp.einsum("bij,bj->bi", jacobian, picked, preferred_element_type=jnp.float32)

    def backward(impulse_field):
        pushes = jnp.einsum(
            "bij,bi->bj", jacobian, impulse_field, preferred_element_type=jnp.float32
        )
        pushes = jnp.transpose(pushes.reshape(blocks, 6, GB), (1, 0, 2))
        nearby = jnp.zeros((6, 9 * grains), jnp.float32).at[:, grain_slots].add(pushes)
        nearby = nearby.reshape(6, 3, 3, grains)
        row_sums = nearby[:, :, 1]
        for step_y in (-1, 1):
            row_sums = row_sums + from_behind(
                nearby[:, :, step_y + 1].astype(jnp.bfloat16), GY, step_y
            ).astype(jnp.float32)
        summed = row_sums[:, 1]
        for step_x in (-1, 1):
            summed = summed + from_behind(row_sums[:, step_x + 1], GX, step_x)
        return summed

    constraint_bias = velocity_bias + forward(free_velocity.astype(jnp.bfloat16))
    extrapolated = impulse_start * live_mask
    previous = extrapolated
    current = extrapolated
    weights = momentum_weights(ITERS)
    for iteration in range(ITERS):
        pushed = backward(extrapolated.astype(jnp.bfloat16))
        moved = inverse_mass * pushed
        totals = lax.psum(
            jnp.stack([jnp.sum(extrapolated * extrapolated), jnp.sum(pushed * moved)]), GX_GY
        )
        size_total, energy_total = totals[0], totals[1]
        gradient = (forward(moved.astype(jnp.bfloat16)) + constraint_bias) * live_mask
        step_size = size_total / (energy_total + epsilon)
        current = project_cone(extrapolated - step_size * gradient, friction) * live_mask
        extrapolated = current + weights[iteration] * (current - previous)
        previous = current
    final_push = backward(current.astype(jnp.bfloat16))
    return (current, free_velocity + inverse_mass * final_push)


def solution(mesh):
    finer = Mesh(mesh.devices.reshape(4, 4, 4, 2), ("gx_0", "gx_1", "gy_0", "gy_1"))
    placed = (
        P(GX_GY, None, None),
        P(GX_GY, None),
        P(GX_GY),
        P(GX_GY, None),
        P(GX_GY, None),
        P(GX_GY, None),
        P(None, GX_GY),
        P(None, GX_GY),
    )
    return jax.shard_map(
        shards,
        mesh=finer,
        in_specs=placed,
        out_specs=(P(GX_GY, None), P(None, GX_GY)),
        check_vma=False,
    )
```

```python
import math

import jax
import jax.numpy as jnp
from jax import lax
from jax.sharding import Mesh
from jax.sharding import PartitionSpec as P


CB = 64
GB = 64
ITERS = 3
GX_GY = ("gx_0", "gx_1", "gy_0", "gy_1")
GX = ("gx_0", "gx_1")
GY = ("gy_0", "gy_1")


epsilon = 1e-06


def with_halo(array, sides, width):
    for axis, dim in sides:
        size, length = (lax.axis_size(axis), array.shape[dim])
        up = [(i, (i + 1) % size) for i in range(size - 1)]
        down = [(j, i) for i, j in up]
        last = lax.slice_in_dim(array, length - width, length, axis=dim)
        leading = lax.slice_in_dim(array, 0, width, axis=dim)
        before = lax.ppermute(last, axis, up)
        after = lax.ppermute(leading, axis, down)
        array = jnp.concatenate([before, array, after], axis=dim)
    return array


def from_behind(block, axis, distance):
    devices = range(lax.axis_size(axis))
    route = [(i - distance, i) for i in devices if i - distance in devices]
    return lax.ppermute(block, axis, route)


def momentum_weights(iterations):
    momentum = 1.0
    weights = []
    for _ in range(iterations):
        upcoming = (-momentum * momentum + momentum * math.sqrt(momentum * momentum + 4.0)) / 2.0
        weights.append(momentum * (1.0 - momentum) / (momentum * momentum + upcoming))
        momentum = upcoming
    return weights


def project_cone(target, friction):
    normal = target[:, :CB]
    tangent_one = target[:, CB : 2 * CB]
    tangent_two = target[:, 2 * CB :]
    tangent_norm = jnp.sqrt(tangent_one * tangent_one + tangent_two * tangent_two)
    inside = tangent_norm <= friction * normal
    opposite = friction * tangent_norm <= -normal
    cone_normal = (normal + friction * tangent_norm) / (1.0 + friction * friction)
    cone_ratio = friction * cone_normal / jnp.where(tangent_norm > 0, tangent_norm, 1.0)
    new_normal = jnp.where(inside, normal, jnp.where(opposite, 0.0, cone_normal))
    shrink = jnp.where(inside, 1.0, jnp.where(opposite, 0.0, cone_ratio))
    return jnp.concatenate([new_normal, tangent_one * shrink, tangent_two * shrink], axis=1)


def shards(
    jacobian,
    grain_slots,
    block_count,
    impulse_start,
    velocity_bias,
    friction,
    free_velocity,
    inverse_mass,
):
    blocks = jacobian.shape[0]
    grains = free_velocity.shape[1]
    live_mask = (jnp.arange(blocks, dtype=jnp.int32) < block_count[0]).astype(jnp.float32)[:, None]

    def forward(grain_field):
        nearby = with_halo(grain_field.reshape(6, 1, 1, grains), ((GX, 1), (GY, 2)), 1)
        nearby = nearby.reshape(6, 9 * grains)
        picked = jnp.take(nearby, grain_slots, axis=1)
        picked = jnp.transpose(picked, (1, 0, 2)).reshape(blocks, 6 * GB)
        return jnp.einsum("bij,bj->bi", jacobian, picked, preferred_element_type=jnp.float32)

    def backward(impulse_field):
        pushes = jnp.einsum(
            "bij,bi->bj", jacobian, impulse_field, preferred_element_type=jnp.float32
        )
        pushes = jnp.transpose(pushes.reshape(blocks, 6, GB), (1, 0, 2))
        nearby = jnp.zeros((6, 9 * grains), jnp.float32).at[:, grain_slots].add(pushes)
        nearby = nearby.reshape(6, 3, 3, grains)
        row_sums = nearby[:, :, 1]
        for step_y in (-1, 1):
            row_sums = row_sums + from_behind(
                nearby[:, :, step_y + 1].astype(jnp.bfloat16), GY, step_y
            ).astype(jnp.float32)
        summed = row_sums[:, 1]
        for step_x in (-1, 1):
            summed = summed + from_behind(row_sums[:, step_x + 1], GX, step_x)
        return summed

    constraint_bias = velocity_bias + forward(free_velocity.astype(jnp.bfloat16))
    extrapolated = impulse_start * live_mask
    previous = extrapolated
    current = extrapolated
    weights = momentum_weights(ITERS)
    for iteration in range(ITERS):
        pushed = backward(extrapolated.astype(jnp.bfloat16))
        moved = inverse_mass * pushed
        partial = jnp.stack([jnp.sum(extrapolated * extrapolated), jnp.sum(pushed * moved)])
        totals = lax.psum(jnp.pad(partial, (0, 16384 - 2)), GX_GY)
        size_total, energy_total = totals[0], totals[1]
        gradient = (forward(moved.astype(jnp.bfloat16)) + constraint_bias) * live_mask
        step_size = size_total / (energy_total + epsilon)
        current = project_cone(extrapolated - step_size * gradient, friction) * live_mask
        extrapolated = current + weights[iteration] * (current - previous)
        previous = current
    final_push = backward(current.astype(jnp.bfloat16))
    return (current, free_velocity + inverse_mass * final_push)


def solution(mesh):
    finer = Mesh(mesh.devices.reshape(4, 4, 4, 2), ("gx_0", "gx_1", "gy_0", "gy_1"))
    placed = (
        P(GX_GY, None, None),
        P(GX_GY, None),
        P(GX_GY),
        P(GX_GY, None),
        P(GX_GY, None),
        P(GX_GY, None),
        P(None, GX_GY),
        P(None, GX_GY),
    )
    return jax.shard_map(
        shards,
        mesh=finer,
        in_specs=placed,
        out_specs=(P(GX_GY, None), P(None, GX_GY)),
        check_vma=False,
    )
```

```python
import math

import jax
import jax.numpy as jnp
from jax import lax
from jax.experimental import pallas as pl
from jax.experimental.pallas import tpu as pltpu
from jax.sharding import Mesh
from jax.sharding import PartitionSpec as P

TILE = 1024


def _gather_kernel(field_ref, idx_ref, out_ref):
    rows, cols = field_ref.shape
    idx = idx_ref[...]
    tile = idx.shape[1]
    high = lax.shift_right_logical(idx, 7)
    low = jnp.bitwise_and(idx, 127)
    pick_col = (lax.broadcasted_iota(jnp.int32, (cols, tile), 0) == high).astype(jnp.bfloat16)
    pick_lane = (lax.broadcasted_iota(jnp.int32, (128, tile), 0) == low).astype(jnp.float32)
    spread = jnp.dot(field_ref[...], pick_col, preferred_element_type=jnp.float32)
    spread = spread.reshape(rows // 128, 128, tile) * pick_lane[None]
    out_ref[...] = jnp.sum(spread, axis=1).astype(out_ref.dtype)


def gather_field(field_t, idx_row):
    rows, cols = field_t.shape
    slots = idx_row.shape[1]
    dofs = rows // 128
    return pl.pallas_call(
        _gather_kernel,
        grid=(slots // TILE,),
        in_specs=[
            pl.BlockSpec((rows, cols), lambda i: (0, 0)),
            pl.BlockSpec((1, TILE), lambda i: (0, i)),
        ],
        out_specs=pl.BlockSpec((dofs, TILE), lambda i: (0, i)),
        out_shape=jax.ShapeDtypeStruct((dofs, slots), field_t.dtype),
    )(field_t, idx_row)


def _scatter_kernel(push_ref, idx_row_ref, idx_col_ref, out_ref):
    @pl.when(pl.program_id(0) == 0)
    def _():
        out_ref[...] = jnp.zeros_like(out_ref)

    rows, cols = out_ref.shape
    push = push_ref[...]
    dofs, tile = push.shape
    low = jnp.bitwise_and(idx_row_ref[...], 127)
    high = lax.shift_right_logical(idx_col_ref[...], 7)
    pick_lane = (lax.broadcasted_iota(jnp.int32, (128, tile), 0) == low).astype(jnp.float32)
    pick_col = (lax.broadcasted_iota(jnp.int32, (tile, cols), 1) == high).astype(jnp.bfloat16)
    spread = (push[:, None, :] * pick_lane[None]).reshape(rows, tile)
    upper = spread.astype(jnp.bfloat16)
    lower = (spread - upper.astype(jnp.float32)).astype(jnp.bfloat16)
    out_ref[...] += jnp.dot(upper, pick_col, preferred_element_type=jnp.float32) + jnp.dot(
        lower, pick_col, preferred_element_type=jnp.float32
    )


def scatter_field(push_t, idx_row, idx_col, cols):
    dofs, slots = push_t.shape
    rows = dofs * 128
    return pl.pallas_call(
        _scatter_kernel,
        grid=(slots // TILE,),
        in_specs=[
            pl.BlockSpec((dofs, TILE), lambda i: (0, i)),
            pl.BlockSpec((1, TILE), lambda i: (0, i)),
            pl.BlockSpec((TILE, 1), lambda i: (i, 0)),
        ],
        out_specs=pl.BlockSpec((rows, cols), lambda i: (0, 0)),
        out_shape=jax.ShapeDtypeStruct((rows, cols), jnp.float32),
        compiler_params=pltpu.CompilerParams(dimension_semantics=("arbitrary",)),
    )(push_t, idx_row, idx_col)

CB = 64
GB = 64
ITERS = 3
GX_GY = ("gx_0", "gx_1", "gy_0", "gy_1")
GX = ("gx_0", "gx_1")
GY = ("gy_0", "gy_1")


epsilon = 1e-06


def with_halo(array, sides, width):
    for axis, dim in sides:
        size, length = (lax.axis_size(axis), array.shape[dim])
        up = [(i, (i + 1) % size) for i in range(size - 1)]
        down = [(j, i) for i, j in up]
        last = lax.slice_in_dim(array, length - width, length, axis=dim)
        leading = lax.slice_in_dim(array, 0, width, axis=dim)
        before = lax.ppermute(last, axis, up)
        after = lax.ppermute(leading, axis, down)
        array = jnp.concatenate([before, array, after], axis=dim)
    return array


def from_behind(block, axis, distance):
    devices = range(lax.axis_size(axis))
    route = [(i - distance, i) for i in devices if i - distance in devices]
    return lax.ppermute(block, axis, route)


def one_axis_at_a_time(array, axes):
    for axis in axes:
        array = lax.psum(array, axis)
    return array


def momentum_weights(iterations):
    momentum = 1.0
    weights = []
    for iteration in range(iterations):
        upcoming = (-momentum * momentum + momentum * math.sqrt(momentum * momentum + 4.0)) / 2.0
        weights.append(momentum * (1.0 - momentum) / (momentum * momentum + upcoming))
        momentum = upcoming
    return weights


def project_cone(target, friction):
    normal = target[:, :CB]
    tangent_one = target[:, CB : 2 * CB]
    tangent_two = target[:, 2 * CB :]
    tangent_norm = jnp.sqrt(tangent_one * tangent_one + tangent_two * tangent_two)
    inside = tangent_norm <= friction * normal
    opposite = friction * tangent_norm <= -normal
    cone_normal = (normal + friction * tangent_norm) / (1.0 + friction * friction)
    cone_ratio = friction * cone_normal / jnp.where(tangent_norm > 0, tangent_norm, 1.0)
    new_normal = jnp.where(inside, normal, jnp.where(opposite, 0.0, cone_normal))
    shrink = jnp.where(inside, 1.0, jnp.where(opposite, 0.0, cone_ratio))
    return jnp.concatenate([new_normal, tangent_one * shrink, tangent_two * shrink], axis=1)


def shards(
    jacobian,
    grain_slots,
    block_count,
    impulse_start,
    velocity_bias,
    friction,
    free_velocity,
    inverse_mass,
):
    blocks = jacobian.shape[0]
    grains = free_velocity.shape[1]
    live_mask = (jnp.arange(blocks, dtype=jnp.int32) < block_count[0]).astype(jnp.float32)[:, None]

    slot_index = grain_slots.reshape(1, blocks * GB)
    slot_column = grain_slots.reshape(blocks * GB, 1)

    def to_tiles(grain_field):
        return jnp.transpose(grain_field.reshape(6, grains // 128, 128), (0, 2, 1))

    def from_tiles(tiles):
        return jnp.transpose(tiles.reshape(6, 128, grains // 128), (0, 2, 1)).reshape(6, grains)

    def forward(grain_field):
        own = to_tiles(grain_field).reshape(6 * 128, 1, 1, grains // 128)
        nearby = with_halo(own, ((GX, 1), (GY, 2)), 1)
        nearby = nearby.reshape(6 * 128, 9 * grains // 128)
        picked = gather_field(nearby, slot_index)
        picked = jnp.transpose(picked.reshape(6, blocks, GB), (1, 0, 2)).reshape(blocks, 6 * GB)
        return jnp.einsum("bij,bj->bi", jacobian, picked, preferred_element_type=jnp.float32)

    def backward(impulse_field):
        pushes = jnp.einsum(
            "bij,bi->bj", jacobian, impulse_field, preferred_element_type=jnp.float32
        )
        pushes = jnp.transpose(pushes.reshape(blocks, 6, GB), (1, 0, 2)).reshape(6, blocks * GB)
        nearby = scatter_field(pushes, slot_index, slot_column, 9 * grains // 128)
        nearby = nearby.reshape(6 * 128, 3, 3, grains // 128)
        row_sums = nearby[:, :, 1]
        for step_y in (-1, 1):
            row_sums = row_sums + from_behind(nearby[:, :, step_y + 1], GY, step_y)
        summed = row_sums[:, 1]
        for step_x in (-1, 1):
            summed = summed + from_behind(row_sums[:, step_x + 1], GX, step_x)
        return from_tiles(summed)

    constraint_bias = velocity_bias + forward(free_velocity.astype(jnp.bfloat16))
    extrapolated = impulse_start * live_mask
    previous = extrapolated
    current = extrapolated
    weights = momentum_weights(ITERS)
    for iteration in range(ITERS):
        pushed = backward(extrapolated.astype(jnp.bfloat16))
        moved = inverse_mass * pushed
        size_total, energy_total = (
            one_axis_at_a_time(jnp.sum(extrapolated * extrapolated), GX_GY),
            one_axis_at_a_time(jnp.sum(pushed * moved), GX_GY),
        )
        gradient = (forward(moved.astype(jnp.bfloat16)) + constraint_bias) * live_mask
        step_size = size_total / (energy_total + epsilon)
        current = project_cone(extrapolated - step_size * gradient, friction) * live_mask
        extrapolated = current + weights[iteration] * (current - previous)
        previous = current
    final_push = backward(current.astype(jnp.bfloat16))
    return (current, free_velocity + inverse_mass * final_push)


def solution(mesh):
    finer = Mesh(mesh.devices.reshape(4, 4, 4, 2), ("gx_0", "gx_1", "gy_0", "gy_1"))
    placed = (
        P(GX_GY, None, None),
        P(GX_GY, None),
        P(GX_GY),
        P(GX_GY, None),
        P(GX_GY, None),
        P(GX_GY, None),
        P(None, GX_GY),
        P(None, GX_GY),
    )
    return jax.shard_map(
        shards,
        mesh=finer,
        in_specs=placed,
        out_specs=(P(GX_GY, None), P(None, GX_GY)),
        check_vma=False,
    )
```

```python
import math

import jax
import jax.numpy as jnp
from jax import lax
from jax.experimental import pallas as pl
from jax.experimental.pallas import tpu as pltpu
from jax.sharding import Mesh
from jax.sharding import PartitionSpec as P

TILE = 1024


def _gather_kernel(field_ref, idx_ref, out_ref):
    rows, cols = field_ref.shape
    idx = idx_ref[...]
    tile = idx.shape[1]
    high = lax.shift_right_logical(idx, 7)
    low = jnp.bitwise_and(idx, 127)
    pick_col = (lax.broadcasted_iota(jnp.int32, (cols, tile), 0) == high).astype(jnp.bfloat16)
    pick_lane = (lax.broadcasted_iota(jnp.int32, (128, tile), 0) == low).astype(jnp.float32)
    spread = jnp.dot(field_ref[...], pick_col, preferred_element_type=jnp.float32)
    spread = spread.reshape(rows // 128, 128, tile) * pick_lane[None]
    out_ref[...] = jnp.sum(spread, axis=1).astype(out_ref.dtype)


def gather_field(field_t, idx_row):
    rows, cols = field_t.shape
    slots = idx_row.shape[1]
    dofs = rows // 128
    return pl.pallas_call(
        _gather_kernel,
        grid=(slots // TILE,),
        in_specs=[
            pl.BlockSpec((rows, cols), lambda i: (0, 0)),
            pl.BlockSpec((1, TILE), lambda i: (0, i)),
        ],
        out_specs=pl.BlockSpec((dofs, TILE), lambda i: (0, i)),
        out_shape=jax.ShapeDtypeStruct((dofs, slots), field_t.dtype),
    )(field_t, idx_row)


def _scatter_kernel(push_ref, idx_ref, out_ref):
    @pl.when(pl.program_id(0) == 0)
    def _():
        out_ref[...] = jnp.zeros_like(out_ref)

    rows, cols = out_ref.shape
    push = push_ref[...]
    dofs, tile = push.shape
    idx = idx_ref[...]
    low = jnp.bitwise_and(idx, 127)
    high = lax.shift_right_logical(idx, 7)
    pick_lane = (lax.broadcasted_iota(jnp.int32, (128, tile), 0) == low).astype(jnp.float32)
    pick_col = (lax.broadcasted_iota(jnp.int32, (cols, tile), 0) == high).astype(jnp.bfloat16)
    spread = (push[:, None, :] * pick_lane[None]).reshape(rows, tile)
    upper = spread.astype(jnp.bfloat16)
    lower = (spread - upper.astype(jnp.float32)).astype(jnp.bfloat16)
    over_slots = (((1,), (1,)), ((), ()))
    out_ref[...] += lax.dot_general(
        upper, pick_col, over_slots, preferred_element_type=jnp.float32
    ) + lax.dot_general(lower, pick_col, over_slots, preferred_element_type=jnp.float32)


def scatter_field(push_t, idx_row, cols):
    dofs, slots = push_t.shape
    rows = dofs * 128
    return pl.pallas_call(
        _scatter_kernel,
        grid=(slots // TILE,),
        in_specs=[
            pl.BlockSpec((dofs, TILE), lambda i: (0, i)),
            pl.BlockSpec((1, TILE), lambda i: (0, i)),
        ],
        out_specs=pl.BlockSpec((rows, cols), lambda i: (0, 0)),
        out_shape=jax.ShapeDtypeStruct((rows, cols), jnp.float32),
        compiler_params=pltpu.CompilerParams(dimension_semantics=("arbitrary",)),
    )(push_t, idx_row)


CB = 64
GB = 64
ITERS = 3
GX = ("gx_0", "gx_1", "gx_2", "gx_3")
GY = ("gy_0", "gy_1", "gy_2")
GX_GY = GX + GY


epsilon = 1e-06


def with_halo(array, sides, width):
    for axis, dim in sides:
        size, length = (lax.axis_size(axis), array.shape[dim])
        up = [(i, (i + 1) % size) for i in range(size - 1)]
        down = [(j, i) for i, j in up]
        last = lax.slice_in_dim(array, length - width, length, axis=dim)
        leading = lax.slice_in_dim(array, 0, width, axis=dim)
        before = lax.ppermute(last, axis, up)
        after = lax.ppermute(leading, axis, down)
        array = jnp.concatenate([before, array, after], axis=dim)
    return array


def from_behind(block, axis, distance):
    devices = range(lax.axis_size(axis))
    route = [(i - distance, i) for i in devices if i - distance in devices]
    return lax.ppermute(block, axis, route)


def one_axis_at_a_time(array, axes):
    for axis in axes:
        array = lax.psum(array, axis)
    return array


def momentum_weights(iterations):
    momentum = 1.0
    weights = []
    for iteration in range(iterations):
        upcoming = (-momentum * momentum + momentum * math.sqrt(momentum * momentum + 4.0)) / 2.0
        weights.append(momentum * (1.0 - momentum) / (momentum * momentum + upcoming))
        momentum = upcoming
    return weights


def project_cone(target, friction):
    normal = target[:, :CB]
    tangent_one = target[:, CB : 2 * CB]
    tangent_two = target[:, 2 * CB :]
    tangent_norm = jnp.sqrt(tangent_one * tangent_one + tangent_two * tangent_two)
    inside = tangent_norm <= friction * normal
    opposite = friction * tangent_norm <= -normal
    cone_normal = (normal + friction * tangent_norm) / (1.0 + friction * friction)
    cone_ratio = friction * cone_normal / jnp.where(tangent_norm > 0, tangent_norm, 1.0)
    new_normal = jnp.where(inside, normal, jnp.where(opposite, 0.0, cone_normal))
    shrink = jnp.where(inside, 1.0, jnp.where(opposite, 0.0, cone_ratio))
    return jnp.concatenate([new_normal, tangent_one * shrink, tangent_two * shrink], axis=1)


def shards(
    jacobian,
    grain_slots,
    block_count,
    impulse_start,
    velocity_bias,
    friction,
    free_velocity,
    inverse_mass,
):
    blocks = jacobian.shape[0]
    grains = free_velocity.shape[1]
    live_mask = (jnp.arange(blocks, dtype=jnp.int32) < block_count[0]).astype(jnp.float32)[:, None]

    slot_index = grain_slots.reshape(1, blocks * GB)

    def to_tiles(grain_field):
        return jnp.transpose(grain_field.reshape(6, grains // 128, 128), (0, 2, 1))

    def from_tiles(tiles):
        return jnp.transpose(tiles.reshape(6, 128, grains // 128), (0, 2, 1)).reshape(6, grains)

    def forward(grain_field):
        own = to_tiles(grain_field).reshape(6 * 128, 1, 1, grains // 128)
        nearby = with_halo(own, ((GX, 1), (GY, 2)), 1)
        nearby = nearby.reshape(6 * 128, 9 * grains // 128)
        picked = gather_field(nearby, slot_index)
        picked = jnp.transpose(picked.reshape(6, blocks, GB), (1, 0, 2)).reshape(blocks, 6 * GB)
        return jnp.einsum("bij,bj->bi", jacobian, picked, preferred_element_type=jnp.float32)

    def backward(impulse_field):
        pushes = jnp.einsum(
            "bij,bi->bj", jacobian, impulse_field, preferred_element_type=jnp.float32
        )
        pushes = jnp.transpose(pushes.reshape(blocks, 6, GB), (1, 0, 2)).reshape(6, blocks * GB)
        nearby = scatter_field(pushes, slot_index, 9 * grains // 128)
        nearby = nearby.reshape(6 * 128, 3, 3, grains // 128)
        row_sums = nearby[:, :, 1]
        for step_y in (-1, 1):
            row_sums = row_sums + from_behind(nearby[:, :, step_y + 1], GY, step_y)
        summed = row_sums[:, 1]
        for step_x in (-1, 1):
            summed = summed + from_behind(row_sums[:, step_x + 1], GX, step_x)
        return from_tiles(summed)

    constraint_bias = velocity_bias + forward(free_velocity.astype(jnp.bfloat16))
    extrapolated = impulse_start * live_mask
    previous = extrapolated
    current = extrapolated
    weights = momentum_weights(ITERS)
    for iteration in range(ITERS):
        pushed = backward(extrapolated.astype(jnp.bfloat16))
        moved = inverse_mass * pushed
        size_total, energy_total = (
            one_axis_at_a_time(jnp.sum(extrapolated * extrapolated), GX_GY),
            one_axis_at_a_time(jnp.sum(pushed * moved), GX_GY),
        )
        gradient = (forward(moved.astype(jnp.bfloat16)) + constraint_bias) * live_mask
        step_size = size_total / (energy_total + epsilon)
        current = project_cone(extrapolated - step_size * gradient, friction) * live_mask
        extrapolated = current + weights[iteration] * (current - previous)
        previous = current
    final_push = backward(current.astype(jnp.bfloat16))
    return (current, free_velocity + inverse_mass * final_push)


def solution(mesh):
    finer = Mesh(mesh.devices.reshape((2,) * len(GX_GY)), GX_GY)
    placed = (
        P(GX_GY, None, None),
        P(GX_GY, None),
        P(GX_GY),
        P(GX_GY, None),
        P(GX_GY, None),
        P(GX_GY, None),
        P(None, GX_GY),
        P(None, GX_GY),
    )
    return jax.shard_map(
        shards,
        mesh=finer,
        in_specs=placed,
        out_specs=(P(GX_GY, None), P(None, GX_GY)),
        check_vma=False,
    )
```

```python
import math

import jax
import jax.numpy as jnp
from jax import lax
from jax.experimental import pallas as pl
from jax.experimental.pallas import tpu as pltpu
from jax.sharding import Mesh
from jax.sharding import PartitionSpec as P

TILE = 1024


def _gather_kernel(field_ref, idx_ref, out_ref):
    rows, cols = field_ref.shape
    idx = idx_ref[...]
    tile = idx.shape[1]
    high = lax.shift_right_logical(idx, 7)
    low = jnp.bitwise_and(idx, 127)
    pick_col = (lax.broadcasted_iota(jnp.int32, (cols, tile), 0) == high).astype(jnp.bfloat16)
    pick_lane = (lax.broadcasted_iota(jnp.int32, (128, tile), 0) == low).astype(jnp.float32)
    spread = jnp.dot(field_ref[...], pick_col, preferred_element_type=jnp.float32)
    spread = spread.reshape(rows // 128, 128, tile) * pick_lane[None]
    out_ref[...] = jnp.sum(spread, axis=1).astype(out_ref.dtype)


def gather_field(field_t, idx_row):
    rows, cols = field_t.shape
    slots = idx_row.shape[1]
    dofs = rows // 128
    return pl.pallas_call(
        _gather_kernel,
        grid=(slots // TILE,),
        in_specs=[
            pl.BlockSpec((rows, cols), lambda i: (0, 0)),
            pl.BlockSpec((1, TILE), lambda i: (0, i)),
        ],
        out_specs=pl.BlockSpec((dofs, TILE), lambda i: (0, i)),
        out_shape=jax.ShapeDtypeStruct((dofs, slots), field_t.dtype),
    )(field_t, idx_row)


def _scatter_kernel(push_ref, idx_ref, out_ref):
    @pl.when(pl.program_id(0) == 0)
    def _():
        out_ref[...] = jnp.zeros_like(out_ref)

    rows, cols = out_ref.shape
    push = push_ref[...]
    dofs, tile = push.shape
    idx = idx_ref[...]
    low = jnp.bitwise_and(idx, 127)
    high = lax.shift_right_logical(idx, 7)
    pick_lane = (lax.broadcasted_iota(jnp.int32, (128, tile), 0) == low).astype(jnp.float32)
    pick_col = (lax.broadcasted_iota(jnp.int32, (cols, tile), 0) == high).astype(jnp.bfloat16)
    spread = (push[:, None, :] * pick_lane[None]).reshape(rows, tile)
    upper = spread.astype(jnp.bfloat16)
    lower = (spread - upper.astype(jnp.float32)).astype(jnp.bfloat16)
    over_slots = (((1,), (1,)), ((), ()))
    out_ref[...] += lax.dot_general(
        upper, pick_col, over_slots, preferred_element_type=jnp.float32
    ) + lax.dot_general(lower, pick_col, over_slots, preferred_element_type=jnp.float32)


def scatter_field(push_t, idx_row, cols):
    dofs, slots = push_t.shape
    rows = dofs * 128
    return pl.pallas_call(
        _scatter_kernel,
        grid=(slots // TILE,),
        in_specs=[
            pl.BlockSpec((dofs, TILE), lambda i: (0, i)),
            pl.BlockSpec((1, TILE), lambda i: (0, i)),
        ],
        out_specs=pl.BlockSpec((rows, cols), lambda i: (0, 0)),
        out_shape=jax.ShapeDtypeStruct((rows, cols), jnp.float32),
        compiler_params=pltpu.CompilerParams(dimension_semantics=("arbitrary",)),
    )(push_t, idx_row)


CB = 64
GB = 64
ITERS = 3
GX_GY = ("gx_0", "gx_1", "gy_0", "gy_1")
GX = ("gx_0", "gx_1")
GY = ("gy_0", "gy_1")


epsilon = 1e-06


def with_halo(array, sides, width):
    for axis, dim in sides:
        size, length = (lax.axis_size(axis), array.shape[dim])
        up = [(i, (i + 1) % size) for i in range(size - 1)]
        down = [(j, i) for i, j in up]
        last = lax.slice_in_dim(array, length - width, length, axis=dim)
        leading = lax.slice_in_dim(array, 0, width, axis=dim)
        before = lax.ppermute(last, axis, up)
        after = lax.ppermute(leading, axis, down)
        array = jnp.concatenate([before, array, after], axis=dim)
    return array


def from_behind(block, axis, distance):
    devices = range(lax.axis_size(axis))
    route = [(i - distance, i) for i in devices if i - distance in devices]
    return lax.ppermute(block, axis, route)


def one_axis_at_a_time(array, axes):
    for axis in axes:
        array = lax.psum(array, axis)
    return array


def momentum_weights(iterations):
    momentum = 1.0
    weights = []
    for iteration in range(iterations):
        upcoming = (-momentum * momentum + momentum * math.sqrt(momentum * momentum + 4.0)) / 2.0
        weights.append(momentum * (1.0 - momentum) / (momentum * momentum + upcoming))
        momentum = upcoming
    return weights


def project_cone(target, friction):
    normal = target[:, :CB]
    tangent_one = target[:, CB : 2 * CB]
    tangent_two = target[:, 2 * CB :]
    tangent_norm = jnp.sqrt(tangent_one * tangent_one + tangent_two * tangent_two)
    inside = tangent_norm <= friction * normal
    opposite = friction * tangent_norm <= -normal
    cone_normal = (normal + friction * tangent_norm) / (1.0 + friction * friction)
    cone_ratio = friction * cone_normal / jnp.where(tangent_norm > 0, tangent_norm, 1.0)
    new_normal = jnp.where(inside, normal, jnp.where(opposite, 0.0, cone_normal))
    shrink = jnp.where(inside, 1.0, jnp.where(opposite, 0.0, cone_ratio))
    return jnp.concatenate([new_normal, tangent_one * shrink, tangent_two * shrink], axis=1)


def shards(
    jacobian,
    grain_slots,
    block_count,
    impulse_start,
    velocity_bias,
    friction,
    free_velocity,
    inverse_mass,
):
    blocks = jacobian.shape[0]
    grains = free_velocity.shape[1]
    live_mask = (jnp.arange(blocks, dtype=jnp.int32) < block_count[0]).astype(jnp.float32)[:, None]

    slot_index = grain_slots.reshape(1, blocks * GB)

    def to_tiles(grain_field):
        return jnp.transpose(grain_field.reshape(6, grains // 128, 128), (0, 2, 1))

    def from_tiles(tiles):
        return jnp.transpose(tiles.reshape(6, 128, grains // 128), (0, 2, 1)).reshape(6, grains)

    def forward(grain_field):
        own = to_tiles(grain_field).reshape(6 * 128, 1, 1, grains // 128)
        nearby = with_halo(own, ((GX, 1), (GY, 2)), 1)
        nearby = nearby.reshape(6 * 128, 9 * grains // 128)
        picked = gather_field(nearby, slot_index)
        picked = jnp.transpose(picked.reshape(6, blocks, GB), (1, 0, 2)).reshape(blocks, 6 * GB)
        return jnp.einsum("bij,bj->bi", jacobian, picked, preferred_element_type=jnp.float32)

    def backward(impulse_field):
        pushes = jnp.einsum(
            "bij,bi->bj", jacobian, impulse_field, preferred_element_type=jnp.float32
        )
        pushes = jnp.transpose(pushes.reshape(blocks, 6, GB), (1, 0, 2)).reshape(6, blocks * GB)
        nearby = scatter_field(pushes, slot_index, 9 * grains // 128)
        nearby = nearby.reshape(6 * 128, 3, 3, grains // 128)
        row_sums = nearby[:, :, 1]
        for step_y in (-1, 1):
            row_sums = row_sums + from_behind(nearby[:, :, step_y + 1], GY, step_y)
        summed = row_sums[:, 1]
        for step_x in (-1, 1):
            summed = summed + from_behind(row_sums[:, step_x + 1], GX, step_x)
        return from_tiles(summed)

    constraint_bias = velocity_bias + forward(free_velocity.astype(jnp.bfloat16))
    extrapolated = impulse_start * live_mask
    previous = extrapolated
    current = extrapolated
    weights = momentum_weights(ITERS)
    for iteration in range(ITERS):
        pushed = backward(extrapolated.astype(jnp.bfloat16))
        moved = inverse_mass * pushed
        size_total, energy_total = (
            one_axis_at_a_time(jnp.sum(extrapolated * extrapolated), GX_GY),
            one_axis_at_a_time(jnp.sum(pushed * moved), GX_GY),
        )
        gradient = (forward(moved.astype(jnp.bfloat16)) + constraint_bias) * live_mask
        step_size = size_total / (energy_total + epsilon)
        current = project_cone(extrapolated - step_size * gradient, friction) * live_mask
        extrapolated = current + weights[iteration] * (current - previous)
        previous = current
    final_push = backward(current.astype(jnp.bfloat16))
    return (current, free_velocity + inverse_mass * final_push)


def solution(mesh):
    finer = Mesh(mesh.devices.reshape(4, 4, 4, 2), ("gx_0", "gx_1", "gy_0", "gy_1"))
    placed = (
        P(GX_GY, None, None),
        P(GX_GY, None),
        P(GX_GY),
        P(GX_GY, None),
        P(GX_GY, None),
        P(GX_GY, None),
        P(None, GX_GY),
        P(None, GX_GY),
    )
    return jax.shard_map(
        shards,
        mesh=finer,
        in_specs=placed,
        out_specs=(P(GX_GY, None), P(None, GX_GY)),
        check_vma=False,
    )
```

```python
import math

import jax
import jax.numpy as jnp
from jax import lax
from jax.experimental import pallas as pl
from jax.experimental.pallas import tpu as pltpu
from jax.sharding import Mesh
from jax.sharding import PartitionSpec as P

TILE = 1024


def _gather_kernel(field_ref, idx_ref, out_ref):
    rows, cols = field_ref.shape
    idx = idx_ref[...]
    tile = idx.shape[1]
    high = lax.shift_right_logical(idx, 7)
    low = jnp.bitwise_and(idx, 127)
    pick_col = (lax.broadcasted_iota(jnp.int32, (cols, tile), 0) == high).astype(jnp.bfloat16)
    pick_lane = (lax.broadcasted_iota(jnp.int32, (128, tile), 0) == low).astype(jnp.float32)
    spread = jnp.dot(field_ref[...], pick_col, preferred_element_type=jnp.float32)
    spread = spread.reshape(rows // 128, 128, tile) * pick_lane[None]
    out_ref[...] = jnp.sum(spread, axis=1).astype(out_ref.dtype)


def gather_field(field_t, idx_row):
    rows, cols = field_t.shape
    slots = idx_row.shape[1]
    dofs = rows // 128
    return pl.pallas_call(
        _gather_kernel,
        grid=(slots // TILE,),
        in_specs=[
            pl.BlockSpec((rows, cols), lambda i: (0, 0)),
            pl.BlockSpec((1, TILE), lambda i: (0, i)),
        ],
        out_specs=pl.BlockSpec((dofs, TILE), lambda i: (0, i)),
        out_shape=jax.ShapeDtypeStruct((dofs, slots), field_t.dtype),
    )(field_t, idx_row)


def _scatter_kernel(push_ref, idx_ref, out_ref):
    @pl.when(pl.program_id(0) == 0)
    def _():
        out_ref[...] = jnp.zeros_like(out_ref)

    rows, cols = out_ref.shape
    push = push_ref[...]
    dofs, tile = push.shape
    idx = idx_ref[...]
    low = jnp.bitwise_and(idx, 127)
    high = lax.shift_right_logical(idx, 7)
    pick_lane = (lax.broadcasted_iota(jnp.int32, (128, tile), 0) == low).astype(jnp.float32)
    pick_col = (lax.broadcasted_iota(jnp.int32, (cols, tile), 0) == high).astype(jnp.bfloat16)
    spread = (push[:, None, :] * pick_lane[None]).reshape(rows, tile)
    upper = spread.astype(jnp.bfloat16)
    lower = (spread - upper.astype(jnp.float32)).astype(jnp.bfloat16)
    over_slots = (((1,), (1,)), ((), ()))
    out_ref[...] += lax.dot_general(
        upper, pick_col, over_slots, preferred_element_type=jnp.float32
    ) + lax.dot_general(lower, pick_col, over_slots, preferred_element_type=jnp.float32)


def scatter_field(push_t, idx_row, cols):
    dofs, slots = push_t.shape
    rows = dofs * 128
    return pl.pallas_call(
        _scatter_kernel,
        grid=(slots // TILE,),
        in_specs=[
            pl.BlockSpec((dofs, TILE), lambda i: (0, i)),
            pl.BlockSpec((1, TILE), lambda i: (0, i)),
        ],
        out_specs=pl.BlockSpec((rows, cols), lambda i: (0, 0)),
        out_shape=jax.ShapeDtypeStruct((rows, cols), jnp.float32),
        compiler_params=pltpu.CompilerParams(dimension_semantics=("arbitrary",)),
    )(push_t, idx_row)


CB = 64
GB = 64
ITERS = 3
GX_GY = ("gx_0", "gx_1", "gy_0", "gy_1")
GX = ("gx_0", "gx_1")
GY = ("gy_0", "gy_1")


epsilon = 1e-06


def with_halo(array, sides, width):
    for axis, dim in sides:
        size, length = (lax.axis_size(axis), array.shape[dim])
        up = [(i, (i + 1) % size) for i in range(size - 1)]
        down = [(j, i) for i, j in up]
        last = lax.slice_in_dim(array, length - width, length, axis=dim)
        leading = lax.slice_in_dim(array, 0, width, axis=dim)
        before = lax.ppermute(last, axis, up)
        after = lax.ppermute(leading, axis, down)
        array = jnp.concatenate([before, array, after], axis=dim)
    return array


def from_behind(block, axis, distance):
    devices = range(lax.axis_size(axis))
    route = [(i - distance, i) for i in devices if i - distance in devices]
    return lax.ppermute(block, axis, route)


def butterfly_sum(array, axes):
    size = 1
    for axis in axes:
        size *= lax.axis_size(axis)
    step = 1
    while step < size:
        array = array + lax.ppermute(array, axes, [(i, i ^ step) for i in range(size)])
        step *= 2
    return array


def momentum_weights(iterations):
    momentum = 1.0
    weights = []
    for iteration in range(iterations):
        upcoming = (-momentum * momentum + momentum * math.sqrt(momentum * momentum + 4.0)) / 2.0
        weights.append(momentum * (1.0 - momentum) / (momentum * momentum + upcoming))
        momentum = upcoming
    return weights


def project_cone(target, friction):
    normal = target[:, :CB]
    tangent_one = target[:, CB : 2 * CB]
    tangent_two = target[:, 2 * CB :]
    tangent_norm = jnp.sqrt(tangent_one * tangent_one + tangent_two * tangent_two)
    inside = tangent_norm <= friction * normal
    opposite = friction * tangent_norm <= -normal
    cone_normal = (normal + friction * tangent_norm) / (1.0 + friction * friction)
    cone_ratio = friction * cone_normal / jnp.where(tangent_norm > 0, tangent_norm, 1.0)
    new_normal = jnp.where(inside, normal, jnp.where(opposite, 0.0, cone_normal))
    shrink = jnp.where(inside, 1.0, jnp.where(opposite, 0.0, cone_ratio))
    return jnp.concatenate([new_normal, tangent_one * shrink, tangent_two * shrink], axis=1)


def shards(
    jacobian,
    grain_slots,
    block_count,
    impulse_start,
    velocity_bias,
    friction,
    free_velocity,
    inverse_mass,
):
    blocks = jacobian.shape[0]
    grains = free_velocity.shape[1]
    live_mask = (jnp.arange(blocks, dtype=jnp.int32) < block_count[0]).astype(jnp.float32)[:, None]

    slot_index = grain_slots.reshape(1, blocks * GB)

    def to_tiles(grain_field):
        return jnp.transpose(grain_field.reshape(6, grains // 128, 128), (0, 2, 1))

    def from_tiles(tiles):
        return jnp.transpose(tiles.reshape(6, 128, grains // 128), (0, 2, 1)).reshape(6, grains)

    def forward(grain_field):
        own = to_tiles(grain_field).reshape(6 * 128, 1, 1, grains // 128)
        nearby = with_halo(own, ((GX, 1), (GY, 2)), 1)
        nearby = nearby.reshape(6 * 128, 9 * grains // 128)
        picked = gather_field(nearby, slot_index)
        picked = jnp.transpose(picked.reshape(6, blocks, GB), (1, 0, 2)).reshape(blocks, 6 * GB)
        return jnp.einsum("bij,bj->bi", jacobian, picked, preferred_element_type=jnp.float32)

    def backward(impulse_field):
        pushes = jnp.einsum(
            "bij,bi->bj", jacobian, impulse_field, preferred_element_type=jnp.float32
        )
        pushes = jnp.transpose(pushes.reshape(blocks, 6, GB), (1, 0, 2)).reshape(6, blocks * GB)
        nearby = scatter_field(pushes, slot_index, 9 * grains // 128)
        nearby = nearby.reshape(6 * 128, 3, 3, grains // 128)
        row_sums = nearby[:, :, 1]
        for step_y in (-1, 1):
            row_sums = row_sums + from_behind(nearby[:, :, step_y + 1], GY, step_y)
        summed = row_sums[:, 1]
        for step_x in (-1, 1):
            summed = summed + from_behind(row_sums[:, step_x + 1], GX, step_x)
        return from_tiles(summed)

    constraint_bias = velocity_bias + forward(free_velocity.astype(jnp.bfloat16))
    extrapolated = impulse_start * live_mask
    previous = extrapolated
    current = extrapolated
    weights = momentum_weights(ITERS)
    for iteration in range(ITERS):
        pushed = backward(extrapolated.astype(jnp.bfloat16))
        moved = inverse_mass * pushed
        totals = butterfly_sum(
            jnp.stack([jnp.sum(extrapolated * extrapolated), jnp.sum(pushed * moved)]), GX_GY
        )
        size_total, energy_total = totals[0], totals[1]
        gradient = (forward(moved.astype(jnp.bfloat16)) + constraint_bias) * live_mask
        step_size = size_total / (energy_total + epsilon)
        current = project_cone(extrapolated - step_size * gradient, friction) * live_mask
        extrapolated = current + weights[iteration] * (current - previous)
        previous = current
    final_push = backward(current.astype(jnp.bfloat16))
    return (current, free_velocity + inverse_mass * final_push)


def solution(mesh):
    finer = Mesh(mesh.devices.reshape(4, 4, 4, 2), ("gx_0", "gx_1", "gy_0", "gy_1"))
    placed = (
        P(GX_GY, None, None),
        P(GX_GY, None),
        P(GX_GY),
        P(GX_GY, None),
        P(GX_GY, None),
        P(GX_GY, None),
        P(None, GX_GY),
        P(None, GX_GY),
    )
    return jax.shard_map(
        shards,
        mesh=finer,
        in_specs=placed,
        out_specs=(P(GX_GY, None), P(None, GX_GY)),
        check_vma=False,
    )
```

```python
import math

import jax
import jax.numpy as jnp
from jax import lax
from jax.experimental import pallas as pl
from jax.experimental.pallas import tpu as pltpu
from jax.sharding import Mesh
from jax.sharding import PartitionSpec as P


TILE = 1024


def _gather_kernel(field_ref, idx_ref, out_ref):
    rows, cols = field_ref.shape
    idx = idx_ref[...]
    tile = idx.shape[1]
    high = lax.shift_right_logical(idx, 7)
    low = jnp.bitwise_and(idx, 127)
    pick_col = (lax.broadcasted_iota(jnp.int32, (cols, tile), 0) == high).astype(jnp.bfloat16)
    pick_lane = (lax.broadcasted_iota(jnp.int32, (128, tile), 0) == low).astype(jnp.float32)
    spread = jnp.dot(field_ref[...], pick_col, preferred_element_type=jnp.float32)
    spread = spread.reshape(rows // 128, 128, tile) * pick_lane[None]
    out_ref[...] = jnp.sum(spread, axis=1).astype(out_ref.dtype)


def gather_field(field_t, idx_row):
    rows, cols = field_t.shape
    slots = idx_row.shape[1]
    dofs = rows // 128
    return pl.pallas_call(
        _gather_kernel,
        grid=(slots // TILE,),
        in_specs=[
            pl.BlockSpec((rows, cols), lambda i: (0, 0)),
            pl.BlockSpec((1, TILE), lambda i: (0, i)),
        ],
        out_specs=pl.BlockSpec((dofs, TILE), lambda i: (0, i)),
        out_shape=jax.ShapeDtypeStruct((dofs, slots), field_t.dtype),
    )(field_t, idx_row)


def _scatter_kernel(push_ref, idx_ref, out_ref):
    @pl.when(pl.program_id(0) == 0)
    def _():
        out_ref[...] = jnp.zeros_like(out_ref)

    rows, cols = out_ref.shape
    push = push_ref[...]
    _, tile = push.shape
    idx = idx_ref[...]
    low = jnp.bitwise_and(idx, 127)
    high = lax.shift_right_logical(idx, 7)
    pick_lane = (lax.broadcasted_iota(jnp.int32, (128, tile), 0) == low).astype(jnp.float32)
    pick_col = (lax.broadcasted_iota(jnp.int32, (cols, tile), 0) == high).astype(jnp.bfloat16)
    spread = (push[:, None, :] * pick_lane[None]).reshape(rows, tile)
    upper = spread.astype(jnp.bfloat16)
    lower = (spread - upper.astype(jnp.float32)).astype(jnp.bfloat16)
    over_slots = (((1,), (1,)), ((), ()))
    out_ref[...] += lax.dot_general(
        upper, pick_col, over_slots, preferred_element_type=jnp.float32
    ) + lax.dot_general(lower, pick_col, over_slots, preferred_element_type=jnp.float32)


def scatter_field(push_t, idx_row, cols):
    dofs, slots = push_t.shape
    rows = dofs * 128
    return pl.pallas_call(
        _scatter_kernel,
        grid=(slots // TILE,),
        in_specs=[
            pl.BlockSpec((dofs, TILE), lambda i: (0, i)),
            pl.BlockSpec((1, TILE), lambda i: (0, i)),
        ],
        out_specs=pl.BlockSpec((rows, cols), lambda i: (0, 0)),
        out_shape=jax.ShapeDtypeStruct((rows, cols), jnp.float32),
        compiler_params=pltpu.CompilerParams(dimension_semantics=("arbitrary",)),
    )(push_t, idx_row)


CB = 64
GB = 64
ITERS = 3
GX_GY = ("gx_0", "gx_1", "gy_0", "gy_1")
GX = ("gx_0", "gx_1")
GY = ("gy_0", "gy_1")


epsilon = 1e-06


def with_halo(array, sides, width):
    for axis, dim in sides:
        size, length = (lax.axis_size(axis), array.shape[dim])
        up = [(i, (i + 1) % size) for i in range(size - 1)]
        down = [(j, i) for i, j in up]
        last = lax.slice_in_dim(array, length - width, length, axis=dim)
        leading = lax.slice_in_dim(array, 0, width, axis=dim)
        before = lax.ppermute(last, axis, up)
        after = lax.ppermute(leading, axis, down)
        array = jnp.concatenate([before, array, after], axis=dim)
    return array


def from_behind(block, axis, distance):
    devices = range(lax.axis_size(axis))
    route = [(i - distance, i) for i in devices if i - distance in devices]
    return lax.ppermute(block, axis, route)


def butterfly_sum(array, axes):
    size = 1
    for axis in axes:
        size *= lax.axis_size(axis)
    step = 1
    while step < size:
        array = array + lax.ppermute(array, axes, [(i, i ^ step) for i in range(size)])
        step = step * 2
    return array


def momentum_weights(iterations):
    momentum = 1.0
    weights = []
    for _ in range(iterations):
        upcoming = (-momentum * momentum + momentum * math.sqrt(momentum * momentum + 4.0)) / 2.0
        weights.append(momentum * (1.0 - momentum) / (momentum * momentum + upcoming))
        momentum = upcoming
    return weights


def project_cone(target, friction):
    normal = target[:, :CB]
    tangent_one = target[:, CB : 2 * CB]
    tangent_two = target[:, 2 * CB :]
    tangent_norm = jnp.sqrt(tangent_one * tangent_one + tangent_two * tangent_two)
    inside = tangent_norm <= friction * normal
    opposite = friction * tangent_norm <= -normal
    cone_normal = (normal + friction * tangent_norm) / (1.0 + friction * friction)
    cone_ratio = friction * cone_normal / jnp.where(tangent_norm > 0, tangent_norm, 1.0)
    new_normal = jnp.where(inside, normal, jnp.where(opposite, 0.0, cone_normal))
    shrink = jnp.where(inside, 1.0, jnp.where(opposite, 0.0, cone_ratio))
    return jnp.concatenate([new_normal, tangent_one * shrink, tangent_two * shrink], axis=1)


def shards(
    jacobian,
    grain_slots,
    block_count,
    impulse_start,
    velocity_bias,
    friction,
    free_velocity,
    inverse_mass,
):
    blocks = jacobian.shape[0]
    grains = free_velocity.shape[1]
    live_mask = (jnp.arange(blocks, dtype=jnp.int32) < block_count[0]).astype(jnp.float32)[:, None]

    slot_index = grain_slots.reshape(1, blocks * GB)

    def to_tiles(grain_field):
        return jnp.transpose(grain_field.reshape(6, grains // 128, 128), (0, 2, 1))

    def from_tiles(tiles):
        return jnp.transpose(tiles.reshape(6, 128, grains // 128), (0, 2, 1)).reshape(6, grains)

    def forward(grain_field):
        own = to_tiles(grain_field).reshape(6 * 128, 1, 1, grains // 128)
        nearby = with_halo(own, ((GX, 1), (GY, 2)), 1)
        nearby = nearby.reshape(6 * 128, 9 * grains // 128)
        picked = gather_field(nearby, slot_index)
        picked = jnp.transpose(picked.reshape(6, blocks, GB), (1, 0, 2)).reshape(blocks, 6 * GB)
        return jnp.einsum("bij,bj->bi", jacobian, picked, preferred_element_type=jnp.float32)

    def backward(impulse_field):
        pushes = jnp.einsum(
            "bij,bi->bj", jacobian, impulse_field, preferred_element_type=jnp.float32
        )
        pushes = jnp.transpose(pushes.reshape(blocks, 6, GB), (1, 0, 2)).reshape(6, blocks * GB)
        nearby = scatter_field(pushes, slot_index, 9 * grains // 128)
        nearby = nearby.reshape(6 * 128, 3, 3, grains // 128)
        row_sums = nearby[:, :, 1]
        for step_y in (-1, 1):
            row_sums = row_sums + from_behind(nearby[:, :, step_y + 1], GY, step_y)
        summed = row_sums[:, 1]
        for step_x in (-1, 1):
            summed = summed + from_behind(row_sums[:, step_x + 1], GX, step_x)
        return from_tiles(summed)

    constraint_bias = velocity_bias + forward(free_velocity.astype(jnp.bfloat16))
    extrapolated = impulse_start * live_mask
    previous = extrapolated
    current = extrapolated
    weights = momentum_weights(ITERS)
    for iteration in range(ITERS):
        pushed = backward(extrapolated.astype(jnp.bfloat16))
        moved = inverse_mass * pushed
        totals = butterfly_sum(
            jnp.stack([jnp.sum(extrapolated * extrapolated), jnp.sum(pushed * moved)]),
            GX_GY,
        )
        size_total, energy_total = totals[0], totals[1]
        gradient = (forward(moved.astype(jnp.bfloat16)) + constraint_bias) * live_mask
        step_size = size_total / (energy_total + epsilon)
        current = project_cone(extrapolated - step_size * gradient, friction) * live_mask
        extrapolated = current + weights[iteration] * (current - previous)
        previous = current
    final_push = backward(current.astype(jnp.bfloat16))
    return (current, free_velocity + inverse_mass * final_push)


def solution(mesh):
    finer = Mesh(mesh.devices.reshape(4, 4, 4, 2), ("gx_0", "gx_1", "gy_0", "gy_1"))
    placed = (
        P(GX_GY, None, None),
        P(GX_GY, None),
        P(GX_GY),
        P(GX_GY, None),
        P(GX_GY, None),
        P(GX_GY, None),
        P(None, GX_GY),
        P(None, GX_GY),
    )
    return jax.shard_map(
        shards,
        mesh=finer,
        in_specs=placed,
        out_specs=(P(GX_GY, None), P(None, GX_GY)),
        check_vma=False,
    )
```

```python
import math

import jax
import jax.numpy as jnp
from jax import lax
from jax.experimental import pallas as pl
from jax.experimental.pallas import tpu as pltpu
from jax.sharding import Mesh
from jax.sharding import PartitionSpec as P


TILE = 1024


def _gather_kernel(field_ref, idx_ref, out_ref):
    rows, cols = field_ref.shape
    idx = idx_ref[...]
    tile = idx.shape[1]
    high = lax.shift_right_logical(idx, 7)
    low = jnp.bitwise_and(idx, 127)
    pick_col = (lax.broadcasted_iota(jnp.int32, (cols, tile), 0) == high).astype(jnp.bfloat16)
    pick_lane = (lax.broadcasted_iota(jnp.int32, (128, tile), 0) == low).astype(jnp.float32)
    spread = jnp.dot(field_ref[...], pick_col, preferred_element_type=jnp.float32)
    spread = spread.reshape(rows // 128, 128, tile) * pick_lane[None]
    out_ref[...] = jnp.sum(spread, axis=1).astype(out_ref.dtype)


def gather_field(field_t, idx_row):
    rows, cols = field_t.shape
    slots = idx_row.shape[1]
    dofs = rows // 128
    return pl.pallas_call(
        _gather_kernel,
        grid=(slots // TILE,),
        in_specs=[
            pl.BlockSpec((rows, cols), lambda i: (0, 0)),
            pl.BlockSpec((1, TILE), lambda i: (0, i)),
        ],
        out_specs=pl.BlockSpec((dofs, TILE), lambda i: (0, i)),
        out_shape=jax.ShapeDtypeStruct((dofs, slots), field_t.dtype),
    )(field_t, idx_row)


def _scatter_kernel(push_ref, idx_ref, out_ref):
    @pl.when(pl.program_id(0) == 0)
    def _():
        out_ref[...] = jnp.zeros_like(out_ref)

    rows, cols = out_ref.shape
    push = push_ref[...]
    _, tile = push.shape
    idx = idx_ref[...]
    low = jnp.bitwise_and(idx, 127)
    high = lax.shift_right_logical(idx, 7)
    pick_lane = (lax.broadcasted_iota(jnp.int32, (128, tile), 0) == low).astype(jnp.float32)
    pick_col = (lax.broadcasted_iota(jnp.int32, (cols, tile), 0) == high).astype(jnp.bfloat16)
    spread = (push[:, None, :] * pick_lane[None]).reshape(rows, tile)
    upper = spread.astype(jnp.bfloat16)
    lower = (spread - upper.astype(jnp.float32)).astype(jnp.bfloat16)
    over_slots = (((1,), (1,)), ((), ()))
    out_ref[...] += lax.dot_general(
        upper, pick_col, over_slots, preferred_element_type=jnp.float32
    ) + lax.dot_general(lower, pick_col, over_slots, preferred_element_type=jnp.float32)


def scatter_field(push_t, idx_row, cols):
    dofs, slots = push_t.shape
    rows = dofs * 128
    return pl.pallas_call(
        _scatter_kernel,
        grid=(slots // TILE,),
        in_specs=[
            pl.BlockSpec((dofs, TILE), lambda i: (0, i)),
            pl.BlockSpec((1, TILE), lambda i: (0, i)),
        ],
        out_specs=pl.BlockSpec((rows, cols), lambda i: (0, 0)),
        out_shape=jax.ShapeDtypeStruct((rows, cols), jnp.float32),
        compiler_params=pltpu.CompilerParams(dimension_semantics=("arbitrary",)),
    )(push_t, idx_row)


CB = 64
GB = 64
ITERS = 3
GX_GY = ("gx_0", "gx_1", "gy_0", "gy_1")
GX = ("gx_0", "gx_1")
GY = ("gy_0", "gy_1")


epsilon = 1e-06


def with_halo(array, sides, width):
    for axis, dim in sides:
        size, length = (lax.axis_size(axis), array.shape[dim])
        up = [(i, (i + 1) % size) for i in range(size - 1)]
        down = [(j, i) for i, j in up]
        last = lax.slice_in_dim(array, length - width, length, axis=dim)
        leading = lax.slice_in_dim(array, 0, width, axis=dim)
        before = lax.ppermute(last, axis, up)
        after = lax.ppermute(leading, axis, down)
        array = jnp.concatenate([before, array, after], axis=dim)
    return array


def from_behind(block, axis, distance):
    devices = range(lax.axis_size(axis))
    route = [(i - distance, i) for i in devices if i - distance in devices]
    return lax.ppermute(block, axis, route)


def exchange_sum(array, axes):
    for axis in axes:
        size = lax.axis_size(axis)
        parts = [array] + [
            lax.ppermute(array, axis, [(i, (i + k) % size) for i in range(size)])
            for k in range(1, size)
        ]
        own = lax.axis_index(axis)
        ordered = []
        for position in range(size):
            chosen = parts[0]
            for k in range(1, size):
                chosen = jnp.where((own - k) % size == position, parts[k], chosen)
            ordered.append(chosen)
        while len(ordered) > 1:
            ordered = [ordered[i] + ordered[i + 1] for i in range(0, len(ordered), 2)]
        array = ordered[0]
    return array


def momentum_weights(iterations):
    momentum = 1.0
    weights = []
    for _ in range(iterations):
        upcoming = (-momentum * momentum + momentum * math.sqrt(momentum * momentum + 4.0)) / 2.0
        weights.append(momentum * (1.0 - momentum) / (momentum * momentum + upcoming))
        momentum = upcoming
    return weights


def project_cone(target, friction):
    normal = target[:, :CB]
    tangent_one = target[:, CB : 2 * CB]
    tangent_two = target[:, 2 * CB :]
    tangent_norm = jnp.sqrt(tangent_one * tangent_one + tangent_two * tangent_two)
    inside = tangent_norm <= friction * normal
    opposite = friction * tangent_norm <= -normal
    cone_normal = (normal + friction * tangent_norm) / (1.0 + friction * friction)
    cone_ratio = friction * cone_normal / jnp.where(tangent_norm > 0, tangent_norm, 1.0)
    new_normal = jnp.where(inside, normal, jnp.where(opposite, 0.0, cone_normal))
    shrink = jnp.where(inside, 1.0, jnp.where(opposite, 0.0, cone_ratio))
    return jnp.concatenate([new_normal, tangent_one * shrink, tangent_two * shrink], axis=1)


def shards(
    jacobian,
    grain_slots,
    block_count,
    impulse_start,
    velocity_bias,
    friction,
    free_velocity,
    inverse_mass,
):
    blocks = jacobian.shape[0]
    grains = free_velocity.shape[1]
    live_mask = (jnp.arange(blocks, dtype=jnp.int32) < block_count[0]).astype(jnp.float32)[:, None]

    slot_index = grain_slots.reshape(1, blocks * GB)

    def to_tiles(grain_field):
        return jnp.transpose(grain_field.reshape(6, grains // 128, 128), (0, 2, 1))

    def from_tiles(tiles):
        return jnp.transpose(tiles.reshape(6, 128, grains // 128), (0, 2, 1)).reshape(6, grains)

    def forward(grain_field):
        own = to_tiles(grain_field).reshape(6 * 128, 1, 1, grains // 128)
        nearby = with_halo(own, ((GX, 1), (GY, 2)), 1)
        nearby = nearby.reshape(6 * 128, 9 * grains // 128)
        picked = gather_field(nearby, slot_index)
        picked = jnp.transpose(picked.reshape(6, blocks, GB), (1, 0, 2)).reshape(blocks, 6 * GB)
        return jnp.einsum("bij,bj->bi", jacobian, picked, preferred_element_type=jnp.float32)

    def backward(impulse_field):
        pushes = jnp.einsum(
            "bij,bi->bj", jacobian, impulse_field, preferred_element_type=jnp.float32
        )
        pushes = jnp.transpose(pushes.reshape(blocks, 6, GB), (1, 0, 2)).reshape(6, blocks * GB)
        nearby = scatter_field(pushes, slot_index, 9 * grains // 128)
        nearby = nearby.reshape(6 * 128, 3, 3, grains // 128)
        row_sums = nearby[:, :, 1]
        for step_y in (-1, 1):
            row_sums = row_sums + from_behind(nearby[:, :, step_y + 1], GY, step_y)
        summed = row_sums[:, 1]
        for step_x in (-1, 1):
            summed = summed + from_behind(row_sums[:, step_x + 1], GX, step_x)
        return from_tiles(summed)

    constraint_bias = velocity_bias + forward(free_velocity.astype(jnp.bfloat16))
    extrapolated = impulse_start * live_mask
    previous = extrapolated
    current = extrapolated
    weights = momentum_weights(ITERS)
    for iteration in range(ITERS):
        pushed = backward(extrapolated.astype(jnp.bfloat16))
        moved = inverse_mass * pushed
        totals = exchange_sum(
            jnp.stack([jnp.sum(extrapolated * extrapolated), jnp.sum(pushed * moved)]),
            ("gy_1", "gy_0", "gx_1", "gx_0"),
        )
        size_total, energy_total = totals[0], totals[1]
        gradient = (forward(moved.astype(jnp.bfloat16)) + constraint_bias) * live_mask
        step_size = size_total / (energy_total + epsilon)
        current = project_cone(extrapolated - step_size * gradient, friction) * live_mask
        extrapolated = current + weights[iteration] * (current - previous)
        previous = current
    final_push = backward(current.astype(jnp.bfloat16))
    return (current, free_velocity + inverse_mass * final_push)


def solution(mesh):
    finer = Mesh(mesh.devices.reshape(4, 4, 4, 2), ("gx_0", "gx_1", "gy_0", "gy_1"))
    placed = (
        P(GX_GY, None, None),
        P(GX_GY, None),
        P(GX_GY),
        P(GX_GY, None),
        P(GX_GY, None),
        P(GX_GY, None),
        P(None, GX_GY),
        P(None, GX_GY),
    )
    return jax.shard_map(
        shards,
        mesh=finer,
        in_specs=placed,
        out_specs=(P(GX_GY, None), P(None, GX_GY)),
        check_vma=False,
    )
```

```python
import math

import jax
import jax.numpy as jnp
from jax import lax
from jax.experimental import pallas as pl
from jax.experimental.pallas import tpu as pltpu
from jax.sharding import Mesh
from jax.sharding import PartitionSpec as P


TILE = 1024


def _gather_kernel(field_ref, idx_ref, out_ref):
    rows, cols = field_ref.shape
    idx = idx_ref[...]
    tile = idx.shape[1]
    high = lax.shift_right_logical(idx, 7)
    low = jnp.bitwise_and(idx, 127)
    pick_col = (lax.broadcasted_iota(jnp.int32, (cols, tile), 0) == high).astype(jnp.bfloat16)
    pick_lane = (lax.broadcasted_iota(jnp.int32, (128, tile), 0) == low).astype(jnp.float32)
    spread = jnp.dot(field_ref[...], pick_col, preferred_element_type=jnp.float32)
    spread = spread.reshape(rows // 128, 128, tile) * pick_lane[None]
    out_ref[...] = jnp.sum(spread, axis=1).astype(out_ref.dtype)


def gather_field(field_t, idx_row):
    rows, cols = field_t.shape
    slots = idx_row.shape[1]
    dofs = rows // 128
    return pl.pallas_call(
        _gather_kernel,
        grid=(slots // TILE,),
        in_specs=[
            pl.BlockSpec((rows, cols), lambda i: (0, 0)),
            pl.BlockSpec((1, TILE), lambda i: (0, i)),
        ],
        out_specs=pl.BlockSpec((dofs, TILE), lambda i: (0, i)),
        out_shape=jax.ShapeDtypeStruct((dofs, slots), field_t.dtype),
    )(field_t, idx_row)


def _scatter_kernel(push_ref, idx_ref, out_ref):
    @pl.when(pl.program_id(0) == 0)
    def _():
        out_ref[...] = jnp.zeros_like(out_ref)

    rows, cols = out_ref.shape
    push = push_ref[...]
    _, tile = push.shape
    idx = idx_ref[...]
    low = jnp.bitwise_and(idx, 127)
    high = lax.shift_right_logical(idx, 7)
    pick_lane = (lax.broadcasted_iota(jnp.int32, (128, tile), 0) == low).astype(jnp.float32)
    pick_col = (lax.broadcasted_iota(jnp.int32, (cols, tile), 0) == high).astype(jnp.bfloat16)
    spread = (push[:, None, :] * pick_lane[None]).reshape(rows, tile)
    upper = spread.astype(jnp.bfloat16)
    lower = (spread - upper.astype(jnp.float32)).astype(jnp.bfloat16)
    over_slots = (((1,), (1,)), ((), ()))
    out_ref[...] += lax.dot_general(
        upper, pick_col, over_slots, preferred_element_type=jnp.float32
    ) + lax.dot_general(lower, pick_col, over_slots, preferred_element_type=jnp.float32)


def scatter_field(push_t, idx_row, cols):
    dofs, slots = push_t.shape
    rows = dofs * 128
    return pl.pallas_call(
        _scatter_kernel,
        grid=(slots // TILE,),
        in_specs=[
            pl.BlockSpec((dofs, TILE), lambda i: (0, i)),
            pl.BlockSpec((1, TILE), lambda i: (0, i)),
        ],
        out_specs=pl.BlockSpec((rows, cols), lambda i: (0, 0)),
        out_shape=jax.ShapeDtypeStruct((rows, cols), jnp.float32),
        compiler_params=pltpu.CompilerParams(dimension_semantics=("arbitrary",)),
    )(push_t, idx_row)


CB = 64
GB = 64
ITERS = 3
GX_GY = ("gx_0", "gx_1", "gy_0", "gy_1")
GX = ("gx_0", "gx_1")
GY = ("gy_0", "gy_1")


epsilon = 1e-06


def with_halo(array, sides, width):
    for axis, dim in sides:
        size, length = (lax.axis_size(axis), array.shape[dim])
        up = [(i, (i + 1) % size) for i in range(size - 1)]
        down = [(j, i) for i, j in up]
        last = lax.slice_in_dim(array, length - width, length, axis=dim)
        leading = lax.slice_in_dim(array, 0, width, axis=dim)
        before = lax.ppermute(last, axis, up)
        after = lax.ppermute(leading, axis, down)
        array = jnp.concatenate([before, array, after], axis=dim)
    return array


def from_behind(block, axis, distance):
    devices = range(lax.axis_size(axis))
    route = [(i - distance, i) for i in devices if i - distance in devices]
    return lax.ppermute(block, axis, route)


def exchange_sum(array, axes):
    for axis in axes:
        size = lax.axis_size(axis)
        parts = [array] + [
            lax.ppermute(array, axis, [(i, (i + k) % size) for i in range(size)])
            for k in range(1, size)
        ]
        ordered = parts
        while len(ordered) > 1:
            half = len(ordered) // 2
            ordered = [ordered[i] + ordered[i + half] for i in range(half)]
        array = ordered[0]
    return array


def momentum_weights(iterations):
    momentum = 1.0
    weights = []
    for _ in range(iterations):
        upcoming = (-momentum * momentum + momentum * math.sqrt(momentum * momentum + 4.0)) / 2.0
        weights.append(momentum * (1.0 - momentum) / (momentum * momentum + upcoming))
        momentum = upcoming
    return weights


def project_cone(target, friction):
    normal = target[:, :CB]
    tangent_one = target[:, CB : 2 * CB]
    tangent_two = target[:, 2 * CB :]
    tangent_norm = jnp.sqrt(tangent_one * tangent_one + tangent_two * tangent_two)
    inside = tangent_norm <= friction * normal
    opposite = friction * tangent_norm <= -normal
    cone_normal = (normal + friction * tangent_norm) / (1.0 + friction * friction)
    cone_ratio = friction * cone_normal / jnp.where(tangent_norm > 0, tangent_norm, 1.0)
    new_normal = jnp.where(inside, normal, jnp.where(opposite, 0.0, cone_normal))
    shrink = jnp.where(inside, 1.0, jnp.where(opposite, 0.0, cone_ratio))
    return jnp.concatenate([new_normal, tangent_one * shrink, tangent_two * shrink], axis=1)


def shards(
    jacobian,
    grain_slots,
    block_count,
    impulse_start,
    velocity_bias,
    friction,
    free_velocity,
    inverse_mass,
):
    blocks = jacobian.shape[0]
    grains = free_velocity.shape[1]
    live_mask = (jnp.arange(blocks, dtype=jnp.int32) < block_count[0]).astype(jnp.float32)[:, None]

    slot_index = grain_slots.reshape(1, blocks * GB)

    def to_tiles(grain_field):
        return jnp.transpose(grain_field.reshape(6, grains // 128, 128), (0, 2, 1))

    def from_tiles(tiles):
        return jnp.transpose(tiles.reshape(6, 128, grains // 128), (0, 2, 1)).reshape(6, grains)

    def forward(grain_field):
        own = to_tiles(grain_field).reshape(6 * 128, 1, 1, grains // 128)
        nearby = with_halo(own, ((GX, 1), (GY, 2)), 1)
        nearby = nearby.reshape(6 * 128, 9 * grains // 128)
        picked = gather_field(nearby, slot_index)
        picked = jnp.transpose(picked.reshape(6, blocks, GB), (1, 0, 2)).reshape(blocks, 6 * GB)
        return jnp.einsum("bij,bj->bi", jacobian, picked, preferred_element_type=jnp.float32)

    def backward(impulse_field):
        pushes = jnp.einsum(
            "bij,bi->bj", jacobian, impulse_field, preferred_element_type=jnp.float32
        )
        pushes = jnp.transpose(pushes.reshape(blocks, 6, GB), (1, 0, 2)).reshape(6, blocks * GB)
        nearby = scatter_field(pushes, slot_index, 9 * grains // 128)
        nearby = nearby.reshape(6 * 128, 3, 3, grains // 128)
        row_sums = nearby[:, :, 1]
        for step_y in (-1, 1):
            row_sums = row_sums + from_behind(nearby[:, :, step_y + 1], GY, step_y)
        summed = row_sums[:, 1]
        for step_x in (-1, 1):
            summed = summed + from_behind(row_sums[:, step_x + 1], GX, step_x)
        return from_tiles(summed)

    constraint_bias = velocity_bias + forward(free_velocity.astype(jnp.bfloat16))
    extrapolated = impulse_start * live_mask
    weights = jnp.asarray(momentum_weights(ITERS), jnp.float32)

    def iteration_step(iteration, carried):
        extrapolated, previous = carried
        pushed = backward(extrapolated.astype(jnp.bfloat16))
        moved = inverse_mass * pushed
        totals = exchange_sum(
            jnp.stack([jnp.sum(extrapolated * extrapolated), jnp.sum(pushed * moved)]),
            ("gy_1", "gy_0", "gx_1", "gx_0"),
        )
        size_total, energy_total = totals[0], totals[1]
        gradient = (forward(moved.astype(jnp.bfloat16)) + constraint_bias) * live_mask
        step_size = size_total / (energy_total + epsilon)
        current = project_cone(extrapolated - step_size * gradient, friction) * live_mask
        return current + weights[iteration] * (current - previous), current

    extrapolated, current = lax.fori_loop(0, ITERS, iteration_step, (extrapolated, extrapolated))
    final_push = backward(current.astype(jnp.bfloat16))
    return (current, free_velocity + inverse_mass * final_push)


def solution(mesh):
    finer = Mesh(mesh.devices.reshape(4, 4, 4, 2), ("gx_0", "gx_1", "gy_0", "gy_1"))
    placed = (
        P(GX_GY, None, None),
        P(GX_GY, None),
        P(GX_GY),
        P(GX_GY, None),
        P(GX_GY, None),
        P(GX_GY, None),
        P(None, GX_GY),
        P(None, GX_GY),
    )
    return jax.shard_map(
        shards,
        mesh=finer,
        in_specs=placed,
        out_specs=(P(GX_GY, None), P(None, GX_GY)),
        check_vma=False,
    )
```

```python
import math

import jax
import jax.numpy as jnp
from jax import lax
from jax.experimental import pallas as pl
from jax.experimental.pallas import tpu as pltpu
from jax.sharding import Mesh
from jax.sharding import PartitionSpec as P


TILE = 1024


def _gather_kernel(field_ref, idx_ref, out_ref):
    rows, cols = field_ref.shape
    idx = idx_ref[...]
    tile = idx.shape[1]
    high = lax.shift_right_logical(idx, 7)
    low = jnp.bitwise_and(idx, 127)
    pick_col = (lax.broadcasted_iota(jnp.int32, (cols, tile), 0) == high).astype(jnp.bfloat16)
    pick_lane = (lax.broadcasted_iota(jnp.int32, (128, tile), 0) == low).astype(jnp.float32)
    spread = jnp.dot(field_ref[...], pick_col, preferred_element_type=jnp.float32)
    spread = spread.reshape(rows // 128, 128, tile) * pick_lane[None]
    out_ref[...] = jnp.sum(spread, axis=1).astype(out_ref.dtype)


def gather_field(field_t, idx_row):
    rows, cols = field_t.shape
    slots = idx_row.shape[1]
    dofs = rows // 128
    return pl.pallas_call(
        _gather_kernel,
        grid=(slots // TILE,),
        in_specs=[
            pl.BlockSpec((rows, cols), lambda i: (0, 0)),
            pl.BlockSpec((1, TILE), lambda i: (0, i)),
        ],
        out_specs=pl.BlockSpec((dofs, TILE), lambda i: (0, i)),
        out_shape=jax.ShapeDtypeStruct((dofs, slots), field_t.dtype),
    )(field_t, idx_row)


def _scatter_kernel(push_ref, idx_ref, out_ref):
    @pl.when(pl.program_id(0) == 0)
    def _():
        out_ref[...] = jnp.zeros_like(out_ref)

    rows, cols = out_ref.shape
    push = push_ref[...]
    _, tile = push.shape
    idx = idx_ref[...]
    low = jnp.bitwise_and(idx, 127)
    high = lax.shift_right_logical(idx, 7)
    pick_lane = (lax.broadcasted_iota(jnp.int32, (128, tile), 0) == low).astype(jnp.float32)
    pick_col = (lax.broadcasted_iota(jnp.int32, (cols, tile), 0) == high).astype(jnp.bfloat16)
    spread = (push[:, None, :] * pick_lane[None]).reshape(rows, tile)
    upper = spread.astype(jnp.bfloat16)
    lower = (spread - upper.astype(jnp.float32)).astype(jnp.bfloat16)
    over_slots = (((1,), (1,)), ((), ()))
    out_ref[...] += lax.dot_general(
        upper, pick_col, over_slots, preferred_element_type=jnp.float32
    ) + lax.dot_general(lower, pick_col, over_slots, preferred_element_type=jnp.float32)


def scatter_field(push_t, idx_row, cols):
    dofs, slots = push_t.shape
    rows = dofs * 128
    return pl.pallas_call(
        _scatter_kernel,
        grid=(slots // TILE,),
        in_specs=[
            pl.BlockSpec((dofs, TILE), lambda i: (0, i)),
            pl.BlockSpec((1, TILE), lambda i: (0, i)),
        ],
        out_specs=pl.BlockSpec((rows, cols), lambda i: (0, 0)),
        out_shape=jax.ShapeDtypeStruct((rows, cols), jnp.float32),
        compiler_params=pltpu.CompilerParams(dimension_semantics=("arbitrary",)),
    )(push_t, idx_row)


CB = 64
GB = 64
ITERS = 3
GX_GY = ("gx_0", "gx_1", "gy_0", "gy_1")
GX = ("gx_0", "gx_1")
GY = ("gy_0", "gy_1")


epsilon = 1e-06


def with_halo(array, sides, width):
    for axis, dim in sides:
        size, length = (lax.axis_size(axis), array.shape[dim])
        up = [(i, (i + 1) % size) for i in range(size - 1)]
        down = [(j, i) for i, j in up]
        last = lax.slice_in_dim(array, length - width, length, axis=dim)
        leading = lax.slice_in_dim(array, 0, width, axis=dim)
        before = lax.ppermute(last, axis, up)
        after = lax.ppermute(leading, axis, down)
        array = jnp.concatenate([before, array, after], axis=dim)
    return array


def from_behind(block, axis, distance):
    devices = range(lax.axis_size(axis))
    route = [(i - distance, i) for i in devices if i - distance in devices]
    return lax.ppermute(block, axis, route)


def exchange_sum(array, axes):
    for axis in axes:
        size = lax.axis_size(axis)
        parts = [array] + [
            lax.ppermute(array, axis, [(i, (i + k) % size) for i in range(size)])
            for k in range(1, size)
        ]
        own = lax.axis_index(axis)
        ordered = []
        for position in range(size):
            chosen = parts[0]
            for k in range(1, size):
                chosen = jnp.where((own - k) % size == position, parts[k], chosen)
            ordered.append(chosen)
        while len(ordered) > 1:
            ordered = [ordered[i] + ordered[i + 1] for i in range(0, len(ordered), 2)]
        array = ordered[0]
    return array


def momentum_weights(iterations):
    momentum = 1.0
    weights = []
    for _ in range(iterations):
        upcoming = (-momentum * momentum + momentum * math.sqrt(momentum * momentum + 4.0)) / 2.0
        weights.append(momentum * (1.0 - momentum) / (momentum * momentum + upcoming))
        momentum = upcoming
    return weights


def project_cone(target, friction):
    normal = target[:, :CB]
    tangent_one = target[:, CB : 2 * CB]
    tangent_two = target[:, 2 * CB :]
    tangent_norm = jnp.sqrt(tangent_one * tangent_one + tangent_two * tangent_two)
    inside = tangent_norm <= friction * normal
    opposite = friction * tangent_norm <= -normal
    cone_normal = (normal + friction * tangent_norm) / (1.0 + friction * friction)
    cone_ratio = friction * cone_normal / jnp.where(tangent_norm > 0, tangent_norm, 1.0)
    new_normal = jnp.where(inside, normal, jnp.where(opposite, 0.0, cone_normal))
    shrink = jnp.where(inside, 1.0, jnp.where(opposite, 0.0, cone_ratio))
    return jnp.concatenate([new_normal, tangent_one * shrink, tangent_two * shrink], axis=1)


def shards(
    jacobian,
    grain_slots,
    block_count,
    impulse_start,
    velocity_bias,
    friction,
    free_velocity,
    inverse_mass,
):
    blocks = jacobian.shape[0]
    grains = free_velocity.shape[1]
    live_mask = (jnp.arange(blocks, dtype=jnp.int32) < block_count[0]).astype(jnp.float32)[:, None]

    slot_index = grain_slots.reshape(1, blocks * GB)

    def to_tiles(grain_field):
        return jnp.transpose(grain_field.reshape(6, grains // 128, 128), (0, 2, 1))

    def from_tiles(tiles):
        return jnp.transpose(tiles.reshape(6, 128, grains // 128), (0, 2, 1)).reshape(6, grains)

    def forward(grain_field):
        own = to_tiles(grain_field).reshape(6 * 128, 1, 1, grains // 128)
        nearby = with_halo(own, ((GX, 1), (GY, 2)), 1)
        nearby = nearby.reshape(6 * 128, 9 * grains // 128)
        picked = gather_field(nearby, slot_index)
        return jnp.einsum(
            "bidj,dbj->bi",
            jacobian.reshape(blocks, 3 * CB, 6, GB),
            picked.reshape(6, blocks, GB),
            preferred_element_type=jnp.float32,
        )

    def backward(impulse_field):
        pushes = jnp.einsum(
            "bij,bi->bj", jacobian, impulse_field, preferred_element_type=jnp.float32
        )
        pushes = jnp.transpose(pushes.reshape(blocks, 6, GB), (1, 0, 2)).reshape(6, blocks * GB)
        nearby = scatter_field(pushes, slot_index, 9 * grains // 128)
        nearby = nearby.reshape(6 * 128, 3, 3, grains // 128)
        row_sums = nearby[:, :, 1]
        for step_y in (-1, 1):
            row_sums = row_sums + from_behind(nearby[:, :, step_y + 1], GY, step_y)
        summed = row_sums[:, 1]
        for step_x in (-1, 1):
            summed = summed + from_behind(row_sums[:, step_x + 1], GX, step_x)
        return from_tiles(summed)

    constraint_bias = velocity_bias + forward(free_velocity.astype(jnp.bfloat16))
    extrapolated = impulse_start * live_mask
    previous = extrapolated
    current = extrapolated
    weights = momentum_weights(ITERS)
    for iteration in range(ITERS):
        pushed = backward(extrapolated.astype(jnp.bfloat16))
        moved = inverse_mass * pushed
        totals = exchange_sum(
            jnp.stack([jnp.sum(extrapolated * extrapolated), jnp.sum(pushed * moved)]),
            ("gy_1", "gy_0", "gx_1", "gx_0"),
        )
        size_total, energy_total = totals[0], totals[1]
        gradient = (forward(moved.astype(jnp.bfloat16)) + constraint_bias) * live_mask
        step_size = size_total / (energy_total + epsilon)
        current = project_cone(extrapolated - step_size * gradient, friction) * live_mask
        extrapolated = current + weights[iteration] * (current - previous)
        previous = current
    final_push = backward(current.astype(jnp.bfloat16))
    return (current, free_velocity + inverse_mass * final_push)


def solution(mesh):
    finer = Mesh(mesh.devices.reshape(4, 4, 4, 2), ("gx_0", "gx_1", "gy_0", "gy_1"))
    placed = (
        P(GX_GY, None, None),
        P(GX_GY, None),
        P(GX_GY),
        P(GX_GY, None),
        P(GX_GY, None),
        P(GX_GY, None),
        P(None, GX_GY),
        P(None, GX_GY),
    )
    return jax.shard_map(
        shards,
        mesh=finer,
        in_specs=placed,
        out_specs=(P(GX_GY, None), P(None, GX_GY)),
        check_vma=False,
    )
```

```python
import math

import jax
import jax.numpy as jnp
from jax import lax
from jax.experimental import pallas as pl
from jax.experimental.pallas import tpu as pltpu
from jax.sharding import Mesh
from jax.sharding import PartitionSpec as P


TILE = 1024


def _gather_kernel(field_ref, idx_ref, out_ref):
    rows, cols = field_ref.shape
    idx = idx_ref[...]
    tile = idx.shape[1]
    high = lax.shift_right_logical(idx, 7)
    low = jnp.bitwise_and(idx, 127)
    pick_col = (lax.broadcasted_iota(jnp.int32, (cols, tile), 0) == high).astype(jnp.bfloat16)
    pick_lane = (lax.broadcasted_iota(jnp.int32, (128, tile), 0) == low).astype(jnp.float32)
    spread = jnp.dot(field_ref[...], pick_col, preferred_element_type=jnp.float32)
    spread = spread.reshape(rows // 128, 128, tile) * pick_lane[None]
    out_ref[...] = jnp.sum(spread, axis=1).astype(out_ref.dtype)


def gather_field(field_t, idx_row):
    rows, cols = field_t.shape
    slots = idx_row.shape[1]
    dofs = rows // 128
    return pl.pallas_call(
        _gather_kernel,
        grid=(slots // TILE,),
        in_specs=[
            pl.BlockSpec((rows, cols), lambda i: (0, 0)),
            pl.BlockSpec((1, TILE), lambda i: (0, i)),
        ],
        out_specs=pl.BlockSpec((dofs, TILE), lambda i: (0, i)),
        out_shape=jax.ShapeDtypeStruct((dofs, slots), field_t.dtype),
    )(field_t, idx_row)


def _scatter_kernel(push_ref, idx_ref, out_ref):
    @pl.when(pl.program_id(0) == 0)
    def _():
        out_ref[...] = jnp.zeros_like(out_ref)

    rows, cols = out_ref.shape
    push = push_ref[...]
    _, tile = push.shape
    idx = idx_ref[...]
    low = jnp.bitwise_and(idx, 127)
    high = lax.shift_right_logical(idx, 7)
    pick_lane = (lax.broadcasted_iota(jnp.int32, (128, tile), 0) == low).astype(jnp.float32)
    pick_col = (lax.broadcasted_iota(jnp.int32, (cols, tile), 0) == high).astype(jnp.bfloat16)
    spread = (push[:, None, :] * pick_lane[None]).reshape(rows, tile)
    upper = spread.astype(jnp.bfloat16)
    lower = (spread - upper.astype(jnp.float32)).astype(jnp.bfloat16)
    over_slots = (((1,), (1,)), ((), ()))
    out_ref[...] += lax.dot_general(
        upper, pick_col, over_slots, preferred_element_type=jnp.float32
    ) + lax.dot_general(lower, pick_col, over_slots, preferred_element_type=jnp.float32)


def scatter_field(push_t, idx_row, cols):
    dofs, slots = push_t.shape
    rows = dofs * 128
    return pl.pallas_call(
        _scatter_kernel,
        grid=(slots // TILE,),
        in_specs=[
            pl.BlockSpec((dofs, TILE), lambda i: (0, i)),
            pl.BlockSpec((1, TILE), lambda i: (0, i)),
        ],
        out_specs=pl.BlockSpec((rows, cols), lambda i: (0, 0)),
        out_shape=jax.ShapeDtypeStruct((rows, cols), jnp.float32),
        compiler_params=pltpu.CompilerParams(dimension_semantics=("arbitrary",)),
    )(push_t, idx_row)


CB = 64
GB = 64
ITERS = 3
GX_GY = ("gx_0", "gx_1", "gy_0", "gy_1")
GX = ("gx_0", "gx_1")
GY = ("gy_0", "gy_1")


epsilon = 1e-06


def with_halo(array, sides, width):
    for axis, dim in sides:
        size, length = (lax.axis_size(axis), array.shape[dim])
        up = [(i, (i + 1) % size) for i in range(size - 1)]
        down = [(j, i) for i, j in up]
        last = lax.slice_in_dim(array, length - width, length, axis=dim)
        leading = lax.slice_in_dim(array, 0, width, axis=dim)
        before = lax.ppermute(last, axis, up)
        after = lax.ppermute(leading, axis, down)
        array = jnp.concatenate([before, array, after], axis=dim)
    return array


def from_behind(block, axis, distance):
    devices = range(lax.axis_size(axis))
    route = [(i - distance, i) for i in devices if i - distance in devices]
    return lax.ppermute(block, axis, route)


def exchange_sum(array, axes):
    for axis in axes:
        size = lax.axis_size(axis)
        parts = [array] + [
            lax.ppermute(array, axis, [(i, (i + k) % size) for i in range(size)])
            for k in range(1, size)
        ]
        ordered = parts
        while len(ordered) > 1:
            half = len(ordered) // 2
            ordered = [ordered[i] + ordered[i + half] for i in range(half)]
        array = ordered[0]
    return array


def momentum_weights(iterations):
    momentum = 1.0
    weights = []
    for _ in range(iterations):
        upcoming = (-momentum * momentum + momentum * math.sqrt(momentum * momentum + 4.0)) / 2.0
        weights.append(momentum * (1.0 - momentum) / (momentum * momentum + upcoming))
        momentum = upcoming
    return weights


def project_cone(target, friction):
    normal = target[:, :CB]
    tangent_one = target[:, CB : 2 * CB]
    tangent_two = target[:, 2 * CB :]
    tangent_norm = jnp.sqrt(tangent_one * tangent_one + tangent_two * tangent_two)
    inside = tangent_norm <= friction * normal
    opposite = friction * tangent_norm <= -normal
    cone_normal = (normal + friction * tangent_norm) / (1.0 + friction * friction)
    cone_ratio = friction * cone_normal / jnp.where(tangent_norm > 0, tangent_norm, 1.0)
    new_normal = jnp.where(inside, normal, jnp.where(opposite, 0.0, cone_normal))
    shrink = jnp.where(inside, 1.0, jnp.where(opposite, 0.0, cone_ratio))
    return jnp.concatenate([new_normal, tangent_one * shrink, tangent_two * shrink], axis=1)


def shards(
    jacobian,
    grain_slots,
    block_count,
    impulse_start,
    velocity_bias,
    friction,
    free_velocity,
    inverse_mass,
):
    blocks = jacobian.shape[0]
    grains = free_velocity.shape[1]
    live_mask = (jnp.arange(blocks, dtype=jnp.int32) < block_count[0]).astype(jnp.float32)[:, None]

    slot_index = grain_slots.reshape(1, blocks * GB)

    def to_tiles(grain_field):
        return jnp.transpose(grain_field.reshape(6, grains // 128, 128), (0, 2, 1))

    def from_tiles(tiles):
        return jnp.transpose(tiles.reshape(6, 128, grains // 128), (0, 2, 1)).reshape(6, grains)

    def forward(grain_field):
        own = to_tiles(grain_field).reshape(6 * 128, 1, 1, grains // 128)
        nearby = with_halo(own, ((GX, 1), (GY, 2)), 1)
        nearby = nearby.reshape(6 * 128, 9 * grains // 128)
        picked = gather_field(nearby, slot_index)
        return jnp.einsum(
            "bidj,dbj->bi",
            jacobian.reshape(blocks, 3 * CB, 6, GB),
            picked.reshape(6, blocks, GB),
            preferred_element_type=jnp.float32,
        )

    def backward(impulse_field):
        pushes = jnp.einsum(
            "bij,bi->bj", jacobian, impulse_field, preferred_element_type=jnp.float32
        )
        pushes = jnp.transpose(pushes.reshape(blocks, 6, GB), (1, 0, 2)).reshape(6, blocks * GB)
        nearby = scatter_field(pushes, slot_index, 9 * grains // 128)
        nearby = nearby.reshape(6 * 128, 3, 3, grains // 128)
        row_sums = nearby[:, :, 1]
        for step_y in (-1, 1):
            row_sums = row_sums + from_behind(nearby[:, :, step_y + 1], GY, step_y)
        summed = row_sums[:, 1]
        for step_x in (-1, 1):
            summed = summed + from_behind(row_sums[:, step_x + 1], GX, step_x)
        return from_tiles(summed)

    constraint_bias = velocity_bias + forward(free_velocity.astype(jnp.bfloat16))
    extrapolated = impulse_start * live_mask
    previous = extrapolated
    current = extrapolated
    weights = momentum_weights(ITERS)
    for iteration in range(ITERS):
        pushed = backward(extrapolated.astype(jnp.bfloat16))
        moved = inverse_mass * pushed
        totals = exchange_sum(
            jnp.stack([jnp.sum(extrapolated * extrapolated), jnp.sum(pushed * moved)]),
            ("gy_1", "gy_0", "gx_1", "gx_0"),
        )
        size_total, energy_total = totals[0], totals[1]
        gradient = (forward(moved.astype(jnp.bfloat16)) + constraint_bias) * live_mask
        step_size = size_total / (energy_total + epsilon)
        current = project_cone(extrapolated - step_size * gradient, friction) * live_mask
        extrapolated = current + weights[iteration] * (current - previous)
        previous = current
    final_push = backward(current.astype(jnp.bfloat16))
    return (current, free_velocity + inverse_mass * final_push)


def solution(mesh):
    finer = Mesh(mesh.devices.reshape(4, 4, 4, 2), ("gx_0", "gx_1", "gy_0", "gy_1"))
    placed = (
        P(GX_GY, None, None),
        P(GX_GY, None),
        P(GX_GY),
        P(GX_GY, None),
        P(GX_GY, None),
        P(GX_GY, None),
        P(None, GX_GY),
        P(None, GX_GY),
    )
    return jax.shard_map(
        shards,
        mesh=finer,
        in_specs=placed,
        out_specs=(P(GX_GY, None), P(None, GX_GY)),
        check_vma=False,
    )
```

```python
import math

import jax
import jax.numpy as jnp
from jax import lax
from jax.experimental import pallas as pl
from jax.experimental.pallas import tpu as pltpu
from jax.sharding import Mesh
from jax.sharding import PartitionSpec as P


TILE = 1024


def _gather_kernel(field_ref, idx_ref, out_ref):
    rows, cols = field_ref.shape
    idx = idx_ref[...]
    tile = idx.shape[1]
    high = lax.shift_right_logical(idx, 7)
    low = jnp.bitwise_and(idx, 127)
    pick_col = (lax.broadcasted_iota(jnp.int32, (cols, tile), 0) == high).astype(jnp.bfloat16)
    pick_lane = (lax.broadcasted_iota(jnp.int32, (128, tile), 0) == low).astype(jnp.float32)
    spread = jnp.dot(field_ref[...], pick_col, preferred_element_type=jnp.float32)
    spread = spread.reshape(rows // 128, 128, tile) * pick_lane[None]
    out_ref[...] = jnp.sum(spread, axis=1).astype(out_ref.dtype)


def gather_field(field_t, idx_row):
    rows, cols = field_t.shape
    slots = idx_row.shape[1]
    dofs = rows // 128
    return pl.pallas_call(
        _gather_kernel,
        grid=(slots // TILE,),
        in_specs=[
            pl.BlockSpec((rows, cols), lambda i: (0, 0)),
            pl.BlockSpec((1, TILE), lambda i: (0, i)),
        ],
        out_specs=pl.BlockSpec((dofs, TILE), lambda i: (0, i)),
        out_shape=jax.ShapeDtypeStruct((dofs, slots), field_t.dtype),
    )(field_t, idx_row)


def _scatter_kernel(push_ref, idx_ref, out_ref):
    @pl.when(pl.program_id(0) == 0)
    def _():
        out_ref[...] = jnp.zeros_like(out_ref)

    rows, cols = out_ref.shape
    push = push_ref[...]
    _, tile = push.shape
    idx = idx_ref[...]
    low = jnp.bitwise_and(idx, 127)
    high = lax.shift_right_logical(idx, 7)
    pick_lane = (lax.broadcasted_iota(jnp.int32, (128, tile), 0) == low).astype(jnp.float32)
    pick_col = (lax.broadcasted_iota(jnp.int32, (cols, tile), 0) == high).astype(jnp.bfloat16)
    spread = (push[:, None, :] * pick_lane[None]).reshape(rows, tile)
    upper = spread.astype(jnp.bfloat16)
    lower = (spread - upper.astype(jnp.float32)).astype(jnp.bfloat16)
    over_slots = (((1,), (1,)), ((), ()))
    out_ref[...] += lax.dot_general(
        upper, pick_col, over_slots, preferred_element_type=jnp.float32
    ) + lax.dot_general(lower, pick_col, over_slots, preferred_element_type=jnp.float32)


def scatter_field(push_t, idx_row, cols):
    dofs, slots = push_t.shape
    rows = dofs * 128
    return pl.pallas_call(
        _scatter_kernel,
        grid=(slots // TILE,),
        in_specs=[
            pl.BlockSpec((dofs, TILE), lambda i: (0, i)),
            pl.BlockSpec((1, TILE), lambda i: (0, i)),
        ],
        out_specs=pl.BlockSpec((rows, cols), lambda i: (0, 0)),
        out_shape=jax.ShapeDtypeStruct((rows, cols), jnp.float32),
        compiler_params=pltpu.CompilerParams(dimension_semantics=("arbitrary",)),
    )(push_t, idx_row)


CB = 64
GB = 64
ITERS = 3
GX_GY = ("gx_0", "gx_1", "gy_0", "gy_1")
GX = ("gx_0", "gx_1")
GY = ("gy_0", "gy_1")


epsilon = 1e-06


def with_halo(array, sides, width):
    for axis, dim in sides:
        size, length = (lax.axis_size(axis), array.shape[dim])
        up = [(i, (i + 1) % size) for i in range(size - 1)]
        down = [(j, i) for i, j in up]
        last = lax.slice_in_dim(array, length - width, length, axis=dim)
        leading = lax.slice_in_dim(array, 0, width, axis=dim)
        before = lax.ppermute(last, axis, up)
        after = lax.ppermute(leading, axis, down)
        array = jnp.concatenate([before, array, after], axis=dim)
    return array


def from_behind(block, axis, distance):
    devices = range(lax.axis_size(axis))
    route = [(i - distance, i) for i in devices if i - distance in devices]
    return lax.ppermute(block, axis, route)


def exchange_sum(array, axes):
    for axis in axes:
        size = lax.axis_size(axis)
        parts = [array] + [
            lax.ppermute(array, axis, [(i, (i + k) % size) for i in range(size)])
            for k in range(1, size)
        ]
        own = lax.axis_index(axis)
        ordered = []
        for position in range(size):
            chosen = parts[0]
            for k in range(1, size):
                chosen = jnp.where((own - k) % size == position, parts[k], chosen)
            ordered.append(chosen)
        while len(ordered) > 1:
            ordered = [ordered[i] + ordered[i + 1] for i in range(0, len(ordered), 2)]
        array = ordered[0]
    return array


def momentum_weights(iterations):
    momentum = 1.0
    weights = []
    for _ in range(iterations):
        upcoming = (-momentum * momentum + momentum * math.sqrt(momentum * momentum + 4.0)) / 2.0
        weights.append(momentum * (1.0 - momentum) / (momentum * momentum + upcoming))
        momentum = upcoming
    return weights


def project_cone(target, friction):
    normal = target[:, :CB]
    tangent_one = target[:, CB : 2 * CB]
    tangent_two = target[:, 2 * CB :]
    tangent_norm = jnp.sqrt(tangent_one * tangent_one + tangent_two * tangent_two)
    inside = tangent_norm <= friction * normal
    opposite = friction * tangent_norm <= -normal
    cone_normal = (normal + friction * tangent_norm) / (1.0 + friction * friction)
    cone_ratio = friction * cone_normal / jnp.where(tangent_norm > 0, tangent_norm, 1.0)
    new_normal = jnp.where(inside, normal, jnp.where(opposite, 0.0, cone_normal))
    shrink = jnp.where(inside, 1.0, jnp.where(opposite, 0.0, cone_ratio))
    return jnp.concatenate([new_normal, tangent_one * shrink, tangent_two * shrink], axis=1)


def shards(
    jacobian,
    grain_slots,
    block_count,
    impulse_start,
    velocity_bias,
    friction,
    free_velocity,
    inverse_mass,
):
    blocks = jacobian.shape[0]
    grains = free_velocity.shape[1]
    live_mask = (jnp.arange(blocks, dtype=jnp.int32) < block_count[0]).astype(jnp.float32)[:, None]

    slot_index = grain_slots.reshape(1, blocks * GB)

    def to_tiles(grain_field):
        return jnp.transpose(grain_field.reshape(6, grains // 128, 128), (0, 2, 1))

    def from_tiles(tiles):
        return jnp.transpose(tiles.reshape(6, 128, grains // 128), (0, 2, 1)).reshape(6, grains)

    def forward(grain_field):
        own = to_tiles(grain_field).reshape(6 * 128, 1, 1, grains // 128)
        nearby = with_halo(own, ((GX, 1), (GY, 2)), 1)
        nearby = nearby.reshape(6 * 128, 9 * grains // 128)
        picked = gather_field(nearby, slot_index)
        return jnp.einsum(
            "bidj,dbj->bi",
            jacobian.reshape(blocks, 3 * CB, 6, GB),
            picked.reshape(6, blocks, GB),
            preferred_element_type=jnp.float32,
        )

    def backward(impulse_field):
        pushes = jnp.einsum(
            "bidj,bi->dbj",
            jacobian.reshape(blocks, 3 * CB, 6, GB),
            impulse_field,
            preferred_element_type=jnp.float32,
        ).reshape(6, blocks * GB)
        nearby = scatter_field(pushes, slot_index, 9 * grains // 128)
        nearby = nearby.reshape(6 * 128, 3, 3, grains // 128)
        row_sums = nearby[:, :, 1]
        for step_y in (-1, 1):
            row_sums = row_sums + from_behind(nearby[:, :, step_y + 1], GY, step_y)
        summed = row_sums[:, 1]
        for step_x in (-1, 1):
            summed = summed + from_behind(row_sums[:, step_x + 1], GX, step_x)
        return from_tiles(summed)

    constraint_bias = velocity_bias + forward(free_velocity.astype(jnp.bfloat16))
    extrapolated = impulse_start * live_mask
    previous = extrapolated
    current = extrapolated
    weights = momentum_weights(ITERS)
    for iteration in range(ITERS):
        pushed = backward(extrapolated.astype(jnp.bfloat16))
        moved = inverse_mass * pushed
        totals = exchange_sum(
            jnp.stack([jnp.sum(extrapolated * extrapolated), jnp.sum(pushed * moved)]),
            ("gy_1", "gy_0", "gx_1", "gx_0"),
        )
        size_total, energy_total = totals[0], totals[1]
        gradient = (forward(moved.astype(jnp.bfloat16)) + constraint_bias) * live_mask
        step_size = size_total / (energy_total + epsilon)
        current = project_cone(extrapolated - step_size * gradient, friction) * live_mask
        extrapolated = current + weights[iteration] * (current - previous)
        previous = current
    final_push = backward(current.astype(jnp.bfloat16))
    return (current, free_velocity + inverse_mass * final_push)


def solution(mesh):
    finer = Mesh(mesh.devices.reshape(4, 4, 4, 2), ("gx_0", "gx_1", "gy_0", "gy_1"))
    placed = (
        P(GX_GY, None, None),
        P(GX_GY, None),
        P(GX_GY),
        P(GX_GY, None),
        P(GX_GY, None),
        P(GX_GY, None),
        P(None, GX_GY),
        P(None, GX_GY),
    )
    return jax.shard_map(
        shards,
        mesh=finer,
        in_specs=placed,
        out_specs=(P(GX_GY, None), P(None, GX_GY)),
        check_vma=False,
    )
```
